32 devices in a mesh: dp: 8 (over z, y), tensor: 4 (over x, core).
Axes of the slice: x: 2, y: 2, z: 4, core: 2. Of those that a mesh axis runs over, the one named last changes fastest.
Arguments:
- hidden: bfloat16 [12288, 1536], P('dp'), may hold values from -6 to 6
- segment_ids: int32 [12288], P('dp'), may hold values from -1 to 12287, as said below
- norm_gain: float32 [1536], replicated, may hold values from 0.5 to 1.5
- gate_weight: bfloat16 [1536, 3072], P(None, 'tensor'), may hold values from -0.15625 to 0.15625
- input_weight: bfloat16 [1536, 3072], P(None, 'tensor'), may hold values from -0.15625 to 0.15625
- step_weight: bfloat16 [1536, 48], P(None, 'tensor'), may hold values from -0.15625 to 0.15625
- state_weight: bfloat16 [1536, 256], replicated, may hold values from -0.15625 to 0.15625
- conv_weight: float32 [4, 3072], P(None, 'tensor'), may hold values from -3 to 3
- state_conv_weight: float32 [4, 256], replicated, may hold values from -3 to 3
- conv_bias: float32 [3072], P('tensor'), may hold values from -0.5 to 0.5
- state_conv_bias: float32 [256], replicated, may hold values from -0.5 to 0.5
- step_bias: float32 [48], P('tensor'), may hold values from -6.9 to -2.25
- decay_log: float32 [48], P('tensor'), may hold values from 0 to 2.77
- skip_gain: float32 [48], P('tensor'), may hold values from 0.5 to 1.5
- gate_norm_gain: float32 [3072], P('tensor'), may hold values from 0.5 to 1.5
- out_weight: bfloat16 [3072, 1536], P('tensor'), may hold values from -0.109375 to 0.109375
- cotangent: bfloat16 [12288, 1536], P('dp'), may hold values from -6 to 6
Outputs:
- block_out: bfloat16 [12288, 1536], P('dp')
- grad_hidden: float32 [12288, 1536], P('dp')
- grad_norm_gain: float32 [1536], replicated
- grad_gate_weight: float32 [1536, 3072], P(None, 'tensor')
- grad_input_weight: float32 [1536, 3072], P(None, 'tensor')
- grad_step_weight: float32 [1536, 48], P(None, 'tensor')
- grad_state_weight: float32 [1536, 256], replicated
- grad_conv_weight: float32 [4, 3072], P(None, 'tensor')
- grad_state_conv_weight: float32 [4, 256], replicated
- grad_conv_bias: float32 [3072], P('tensor')
- grad_state_conv_bias: float32 [256], replicated
- grad_step_bias: float32 [48], P('tensor')
- grad_decay_log: float32 [48], P('tensor')
- grad_skip_gain: float32 [48], P('tensor')
- grad_gate_norm_gain: float32 [3072], P('tensor')
- grad_out_weight: float32 [3072, 1536], P('tensor')
The draws below stay inside these ranges and needn't reach their ends.
Inputs may be any that keep to these rules, and one draw needn't show every extreme that they name: `segment_ids`: each value is -1 for an empty slot or the global index of the first slot of its sequence; a sequence lies within the 1536 slots of one dp index, its slots are consecutive; the empty slots of a dp index come after all its sequences and number a multiple of 256; the last dp index has no empty slot, and the last slot of all starts a sequence of one token.
All inputs are finite; a program needn't handle non-finite values.
Results may differ from the reference program's by a relative error of at most 0.0096.
Values may be sent and summed in bfloat16 or wider, within the bound.
No kernel may reach another device: no remote copies, remote signals or barrier semaphores. Data moves between devices by JAX's collectives and lax.ppermute only.
A program may use at most 256 MiB of HBM per device.

```python
from functools import partial
import jax
import jax.numpy as jnp
from jax import lax

D = 1536
INNER = 3072
HEADS = 48
STATE = 128
CONV = 4
GROUP = 256
TOK_DEV = 1536
TOKENS = 12288
N_DP = 8


def draw_segment_ids(key, part):
    first_key, second_key, third_key = jax.random.split(key, 3)
    padding = jax.random.randint(first_key, (N_DP,), 1, TOK_DEV // (2 * GROUP) + 1)
    filled = jax.random.randint(second_key, (), 0, N_DP)
    devices = jnp.arange(N_DP, dtype=jnp.int32)
    full_rows = (devices == filled) | (devices == N_DP - 1)
    used = jnp.where(full_rows, TOK_DEV, TOK_DEV - GROUP * padding)
    position = jnp.arange(TOK_DEV, dtype=jnp.int32)
    final_slot = (devices == N_DP - 1)[:, None] & (position == TOK_DEV - 1)[None, :]
    starting = (jax.random.randint(third_key, (N_DP, TOK_DEV), 0, GROUP) == 0) | (position == 0)[None, :] | final_slot
    global_pos = devices[:, None] * TOK_DEV + position[None, :]
    marks = jnp.where(starting, global_pos, -1)
    segments = lax.cummax(marks, axis=1)
    segments = jnp.where(position[None, :] < used[:, None], segments, -1)
    return segments.reshape(-1).astype(jnp.int32)


def level_of(own_key, shape, shards, smallest, largest):
    gain, own = 1.0, jax.random.fold_in(own_key, 6)
    for dim, parts in shards:
        steps = jnp.exp(jax.random.uniform(jax.random.fold_in(own, dim), (parts,), jnp.float32, smallest / len(shards), largest / len(shards)))
        gain = gain * jnp.repeat(steps, shape[dim] // parts).reshape([-1 if axis == dim else 1 for axis in range(len(shape))])
    return gain


def gaussian(rng, dims, spread, bound, cuts=(), kind=jnp.bfloat16):
    gain = level_of(rng, dims, cuts, -0.22, 0.18) if cuts else 1.0
    array = jax.random.normal(rng, dims, jnp.float32) * spread * gain
    return jnp.minimum(jnp.maximum(array, -bound), bound).astype(kind)


def setup_inputs(seed: int = 0) -> dict:
    splits = jax.random.split(jax.random.key(seed), 18)
    return {
        "hidden": gaussian(splits[0], (TOKENS, D), 1.0, 6.0, ((0, 8),)),
        "segment_ids": draw_segment_ids(jax.random.fold_in(splits[17], 71), 0),
        "norm_gain": jnp.clip(1.0 + 0.1 * jax.random.normal(splits[2], (D,), jnp.float32), 0.5, 1.5),
        "gate_weight": gaussian(splits[3], (D, INNER), D ** -0.5, 0.15625, ((1, 4),)),
        "input_weight": gaussian(splits[4], (D, INNER), D ** -0.5, 0.15625, ((1, 4),)),
        "step_weight": gaussian(splits[5], (D, HEADS), D ** -0.5, 0.15625, ((1, 4),)),
        "state_weight": gaussian(splits[6], (D, 2 * STATE), D ** -0.5, 0.15625),
        "conv_weight": gaussian(splits[7], (CONV, INNER), CONV ** -0.5, 3.0, ((1, 4),), jnp.float32),
        "state_conv_weight": gaussian(splits[8], (CONV, 2 * STATE), CONV ** -0.5, 3.0, (), jnp.float32),
        "conv_bias": jnp.clip(jax.random.uniform(splits[9], (INNER,), jnp.float32, -0.5, 0.5) * level_of(splits[9], (INNER,), ((0, 4),), -0.4, 0.0), -0.5, 0.5),
        "state_conv_bias": jnp.clip(jax.random.uniform(splits[10], (2 * STATE,), jnp.float32, -0.5, 0.5), -0.5, 0.5),
        "step_bias": jnp.clip(-6.9 + 4.65 * jax.random.uniform(splits[11], (HEADS,), jnp.float32) ** level_of(splits[11], (HEADS,), ((0, 4),), -0.2, 0.2), -6.9, -2.25),
        "decay_log": jnp.clip(2.77 * jax.random.uniform(splits[12], (HEADS,), jnp.float32) ** level_of(splits[12], (HEADS,), ((0, 4),), -0.2, 0.2), 0.0, 2.77),
        "skip_gain": jnp.clip(0.5 + 1.0 * jax.random.uniform(splits[13], (HEADS,), jnp.float32) ** level_of(splits[13], (HEADS,), ((0, 4),), -0.2, 0.2), 0.5, 1.5),
        "gate_norm_gain": jnp.clip(1.0 + 0.1 * jax.random.normal(splits[14], (INNER,), jnp.float32), 0.5, 1.5),
        "out_weight": gaussian(splits[15], (INNER, D), INNER ** -0.5, 0.109375, ((0, 4),)),
        "cotangent": gaussian(splits[16], (TOKENS, D), 1.0, 6.0, ((0, 8),)),
    }


EPS = 1e-05
HIGH = lax.Precision.HIGHEST

def conv_silu(inputs, weights, biases, segments):
    summed = biases[None, :] + weights[0][None, :] * inputs
    for offset in range(1, weights.shape[0]):
        shifted = jnp.concatenate([jnp.zeros((offset, inputs.shape[1]), inputs.dtype), inputs[:-offset]], axis=0)
        seg_shift = jnp.concatenate([jnp.full((offset,), -2, jnp.int32), segments[:-offset].astype(jnp.int32)])
        keeping = (seg_shift == segments.astype(jnp.int32)).astype(inputs.dtype)
        summed = summed + weights[offset][None, :] * shifted * keeping[:, None]
    return jax.nn.silu(summed)

def ssd_scan(values, states, step_raw, step_bias, decay_log, skip_gain, segments, group):
    length = values.shape[0]
    heads = step_bias.shape[0]
    width = values.shape[1] // heads
    state = states.shape[1] // 2
    blocks = length // group
    step = jax.nn.softplus(step_raw + step_bias[None, :])
    rate = step * (-jnp.exp(decay_log))[None, :]
    x_blk = values.reshape(blocks, group, heads, width)
    b_blk = states[:, :state].reshape(blocks, group, state)
    c_blk = states[:, state:].reshape(blocks, group, state)
    step_h = step.reshape(blocks, group, heads).transpose(0, 2, 1)
    cum_h = jnp.cumsum(rate.reshape(blocks, group, heads), axis=1).transpose(0, 2, 1)
    seg_blk = segments.astype(jnp.int32).reshape(blocks, group)
    causal = jnp.tril(jnp.ones((group, group), bool))
    same = ((seg_blk[:, :, None] == seg_blk[:, None, :]) & causal[None])[:, None]
    differ = cum_h[:, :, :, None] - cum_h[:, :, None, :]
    decay = jnp.where(same, jnp.exp(jnp.where(same, differ, 0.0)), 0.0)
    inner_cb = jnp.einsum('cin,cjn->cij', c_blk, b_blk, precision=HIGH)
    mixing = decay * inner_cb[:, None] * step_h[:, :, None, :]
    y_diag = jnp.einsum('chij,cjhp->cihp', mixing, x_blk, precision=HIGH)
    last_seg = seg_blk[:, -1]
    to_end = jnp.exp(cum_h[:, :, -1:] - cum_h) * step_h * (seg_blk == last_seg[:, None])[:, None, :]
    weighted = to_end.transpose(0, 2, 1)[..., None] * x_blk
    local_state = jnp.einsum('cjn,cjhp->chnp', b_blk, weighted, precision=HIGH)
    prev_seg = jnp.concatenate([jnp.full((1,), -3, jnp.int32), last_seg[:-1]])
    carry_keep = (last_seg == prev_seg).astype(values.dtype)[:, None] * jnp.exp(cum_h[:, :, -1])

    def advance(entering, pieces):
        local_part, factor = pieces
        return (local_part + factor[:, None, None] * entering, entering)
    start_state = jnp.zeros((heads, state, width), values.dtype)
    _, entering_all = lax.scan(advance, start_state, (local_state, carry_keep))
    reach = jnp.exp(cum_h).transpose(0, 2, 1) * (seg_blk == prev_seg[:, None])[..., None]
    y_off = jnp.einsum('cin,chnp->cihp', c_blk, entering_all, precision=HIGH) * reach[..., None]
    result = y_diag + y_off + skip_gain[None, None, :, None] * x_blk
    return result.reshape(length, heads * width)

def cross_dot(left, right):
    return lax.dot_general(left, right, (((0,), (0,)), ((), ())), preferred_element_type=jnp.float32)

def back_dot(left, right):
    return lax.dot_general(left, right, (((1,), (1,)), ((), ())), preferred_element_type=jnp.float32)

def reference(hidden, segment_ids, norm_gain, gate_weight, input_weight, step_weight, state_weight, conv_weight, state_conv_weight, conv_bias, state_conv_bias, step_bias, decay_log, skip_gain, gate_norm_gain, out_weight, cotangent):

    def one_block(totals, pieces):
        hid_blk, seg_blk, cot_blk = pieces
        valid = (seg_blk >= 0).astype(jnp.float32)[:, None]
        hidden_f = hid_blk.astype(jnp.float32)
        inverse = lax.rsqrt(lax.optimization_barrier(jnp.mean(hidden_f * hidden_f, axis=1, keepdims=True)) + EPS)
        normed = (hidden_f * inverse * norm_gain[None, :]).astype(jnp.bfloat16)
        gate_pre = jnp.dot(normed, gate_weight, preferred_element_type=jnp.float32)
        input_pre = jnp.dot(normed, input_weight, preferred_element_type=jnp.float32)
        step_pre = jnp.dot(normed, step_weight, preferred_element_type=jnp.float32)
        state_pre = jnp.dot(normed, state_weight, preferred_element_type=jnp.float32)
        conv_out, conv_back = jax.vjp(partial(conv_silu, segments=seg_blk), input_pre, conv_weight, conv_bias)
        state_out, state_back = jax.vjp(partial(conv_silu, segments=seg_blk), state_pre, state_conv_weight, state_conv_bias)
        values_f = lax.optimization_barrier(conv_out.astype(jnp.bfloat16)).astype(jnp.float32)
        states_f = lax.optimization_barrier(state_out.astype(jnp.bfloat16)).astype(jnp.float32)
        mixed_y, ssd_back = jax.vjp(partial(ssd_scan, segments=seg_blk, group=GROUP), values_f, states_f, step_pre, step_bias, decay_log, skip_gain)
        gate_act = jax.nn.silu(gate_pre)
        gated = mixed_y * gate_act
        gate_inverse = lax.rsqrt(lax.optimization_barrier(jnp.mean(gated * gated, axis=1, keepdims=True)) + EPS)
        gnormed = (gated * gate_inverse * gate_norm_gain[None, :]).astype(jnp.bfloat16)
        mix = jnp.dot(gnormed, out_weight, preferred_element_type=jnp.float32)
        block_out = (hidden_f + valid * mix).astype(jnp.bfloat16)
        dmix = (cot_blk.astype(jnp.float32) * valid).astype(jnp.bfloat16)
        g_out = cross_dot(gnormed, dmix)
        d_gn = back_dot(dmix, out_weight)
        g_gnorm = lax.optimization_barrier(jnp.sum(d_gn * gated * gate_inverse, axis=0))
        scaled = d_gn * gate_norm_gain[None, :]
        dotted = lax.optimization_barrier(jnp.mean(gated * scaled, axis=1, keepdims=True))
        d_gated = gate_inverse * scaled - gated * gate_inverse ** 3 * dotted
        d_y = d_gated * gate_act
        sigma = jax.nn.sigmoid(gate_pre)
        d_gate = d_gated * mixed_y * sigma * (1.0 + gate_pre * (1.0 - sigma))
        d_values, d_states, d_step, g_sbias, g_decay, g_skip = ssd_back(d_y)
        d_input, g_conv, g_cbias = conv_back(d_values)
        d_state_pre, g_sconv, g_scbias = state_back(d_states)
        gate_b = d_gate.astype(jnp.bfloat16)
        input_b = d_input.astype(jnp.bfloat16)
        step_b = d_step.astype(jnp.bfloat16)
        state_b = d_state_pre.astype(jnp.bfloat16)
        d_normed = back_dot(gate_b, gate_weight) + back_dot(input_b, input_weight) + back_dot(step_b, step_weight) + back_dot(state_b, state_weight)
        g_norm = lax.optimization_barrier(jnp.sum(d_normed * hidden_f * inverse, axis=0))
        scaled_in = d_normed * norm_gain[None, :]
        grad_h = cot_blk.astype(jnp.float32) + inverse * scaled_in - hidden_f * inverse ** 3 * lax.optimization_barrier(jnp.mean(hidden_f * scaled_in, axis=1, keepdims=True))
        adds = (g_norm, cross_dot(normed, gate_b), cross_dot(normed, input_b), cross_dot(normed, step_b), cross_dot(normed, state_b), g_conv, g_sconv, g_cbias, g_scbias, g_sbias, g_decay, g_skip, g_gnorm, g_out)
        return (tuple((prior + extra for prior, extra in zip(totals, adds))), (block_out, grad_h))
    shapes = (norm_gain.shape, gate_weight.shape, input_weight.shape, step_weight.shape, state_weight.shape, conv_weight.shape, state_conv_weight.shape, conv_bias.shape, state_conv_bias.shape, step_bias.shape, decay_log.shape, skip_gain.shape, gate_norm_gain.shape, out_weight.shape)
    initial = tuple((jnp.zeros(shape, jnp.float32) for shape in shapes))
    pieces = (hidden.reshape(N_DP, TOK_DEV, D), segment_ids.reshape(N_DP, TOK_DEV), cotangent.reshape(N_DP, TOK_DEV, D))
    totals, (outputs, grads_h) = lax.scan(one_block, initial, pieces)
    return (outputs.reshape(TOKENS, D), grads_h.reshape(TOKENS, D), totals[0], totals[1], totals[2], totals[3], totals[4], totals[5], totals[6], totals[7], totals[8], totals[9], totals[10], totals[11], totals[12], totals[13])
```

```python
from functools import partial

import jax
import jax.numpy as jnp
from jax import lax
from jax.experimental import pallas as pl
from jax.experimental.pallas import tpu as pltpu
from jax.sharding import PartitionSpec as P


GROUP = 256
LANES = 128
EPS = 1e-05
LOG2E = 1.4426950408889634
F32 = jnp.float32
BF16 = jnp.bfloat16

NN = (((1,), (0,)), ((), ()))
NT = (((1,), (1,)), ((), ()))
TN = (((0,), (0,)), ((), ()))


def mm(left, right, dims=NN):
    return lax.dot_general(left, right, dims, preferred_element_type=F32)


def halves(v):
    high = v.astype(BF16)
    return high, (v - high.astype(F32)).astype(BF16)


def thirds(v):
    high = v.astype(BF16)
    rest = v - high.astype(F32)
    mid = rest.astype(BF16)
    return high, mid, (rest - mid.astype(F32)).astype(BF16)


def expand(v, onehot):
    high, low = halves(v)
    return mm(high, onehot) + mm(low, onehot)


def head_sum(v, onehot):
    high, low = halves(v)
    return mm(high, onehot, NT) + mm(low, onehot, NT)


def head_onehot(channels, width, base=0):
    lane = lax.broadcasted_iota(jnp.int32, (LANES, channels), 0)
    chan = lax.broadcasted_iota(jnp.int32, (LANES, channels), 1)
    return (lane == base + chan // width).astype(F32).astype(BF16)


def step_terms(step_pre, seg_col, head_row, last_seg, prev_seg, group):
    raw = step_pre + head_row[0:1, :]
    step = jnp.maximum(raw, 0.0) + jnp.log1p(jnp.exp(-jnp.abs(raw)))
    rate2 = step * head_row[1:2, :]
    row = lax.broadcasted_iota(jnp.int32, (group, group), 0)
    col = lax.broadcasted_iota(jnp.int32, (group, group), 1)
    lower = (row >= col).astype(F32).astype(BF16)
    cum = sum(mm(lower, part) for part in thirds(rate2))
    last = cum[group - 1 : group, :]
    reach = jnp.where(seg_col == prev_seg, jnp.exp2(cum), 0.0)
    to_end = jnp.where(seg_col == last_seg, jnp.exp2(jnp.minimum(last - cum, 0.0)), 0.0)
    keep = jnp.exp2(last) * (last_seg == prev_seg).astype(F32)
    return raw, step, cum, reach, to_end, keep


def block_segments(seg_s, block, group):
    last = seg_s[block * group + group - 1].astype(F32)
    prev_at = jnp.maximum(block * group - 1, 0)
    prev = jnp.where(block > 0, seg_s[prev_at].astype(F32), -3.0)
    return last, prev


def forward_kernel(
    dims,
    seg_s, hid, seg_row, cot, norm_gain, gate_w, input_w, state_w, step_w,
    conv_w, conv_b, sconv_w, sconv_b, head_row, gng, out_w,
    normed_o, gate_o, u_o, z_o, sz_o, su_o, st_o, step_o, y_o, sin_o, dgn_o, sums_o,
    ubuf, vbuf, segbuf, carry, cum_t, cum_s, gram, xs_s,
):
    group, channels, _, width, state = dims
    block = pl.program_id(0)
    tiles = channels // LANES
    last_seg, prev_seg = block_segments(seg_s, block, group)

    @pl.when(block == 0)
    def _():
        ubuf[0:8, :] = jnp.zeros((8, channels), F32)
        vbuf[0:8, :] = jnp.zeros((8, 2 * state), F32)
        segbuf[0:8, :] = jnp.full((8, LANES), -2.0, F32)
        carry[...] = jnp.zeros_like(carry)

    h = hid[...].astype(F32)
    inverse = lax.rsqrt(jnp.mean(h * h, axis=1, keepdims=True) + EPS)
    normed = (h * inverse * norm_gain[...]).astype(BF16)
    normed_o[...] = normed
    step_pre = mm(normed, step_w[...])
    step_o[...] = step_pre
    ubuf[8:, :] = mm(normed, input_w[...])
    vbuf[8:, :] = mm(normed, state_w[...])
    gate_o[...] = mm(normed, gate_w[...])

    seg_mat = jnp.broadcast_to(seg_row[...], (group, group))
    seg_full = seg_mat.T
    seg_col = seg_full[:, :LANES]
    segbuf[8:, :] = seg_col
    valid = (seg_col >= 0.0).astype(F32)
    same = [(segbuf[8 - k : 8 - k + group, :] == seg_col).astype(F32) for k in range(1, 4)]

    _, step, cum, reach, to_end, keep = step_terms(
        step_pre, seg_col, head_row[...], last_seg, prev_seg, group
    )
    cum_s[...] = cum
    cum_t[...] = cum.T
    onehot = head_onehot(channels, width)

    for c in range(2 * state // LANES):
        s = slice(c * LANES, (c + 1) * LANES)
        z = sconv_b[:, s] + sconv_w[0:1, s] * vbuf[8:, s]
        for k in range(1, 4):
            z = z + sconv_w[k : k + 1, s] * (vbuf[8 - k : 8 - k + group, s] * same[k - 1])
        sz_o[:, s] = z
        su_o[:, s] = vbuf[8:, s]
        st_o[:, s] = (z * jax.nn.sigmoid(z)).astype(BF16)
    b_mat = st_o[:, :state]
    c_mat = st_o[:, state:]

    row = lax.broadcasted_iota(jnp.int32, (group, group), 0)
    col = lax.broadcasted_iota(jnp.int32, (group, group), 1)
    gram[...] = jnp.where((seg_full == seg_mat) & (row >= col), mm(c_mat, b_mat, NT), 0.0)

    sin_o[...] = carry[...]
    entering = carry[...].astype(BF16)
    b_t = b_mat.T
    lane = lax.broadcasted_iota(jnp.int32, (group, LANES), 1)
    half = group // 2
    square = jnp.zeros((group, LANES), F32)
    dotted = jnp.zeros((group, LANES), F32)
    keep_rows = jnp.broadcast_to(keep, (8, LANES))
    skip_rows = jnp.broadcast_to(head_row[2:3, :], (8, LANES))
    for c in range(tiles):
        s = slice(c * LANES, (c + 1) * LANES)
        hot = onehot[:, s]
        z = conv_b[:, s] + conv_w[0:1, s] * ubuf[8:, s]
        for k in range(1, 4):
            z = z + conv_w[k : k + 1, s] * (ubuf[8 - k : 8 - k + group, s] * same[k - 1])
        z_o[:, s] = z
        u_o[:, s] = ubuf[8:, s].astype(BF16)
        x = (z * jax.nn.sigmoid(z)).astype(BF16).astype(F32)
        xs = (expand(step, hot) * x).astype(BF16)
        xs_s[:, s] = xs
        weighted = (expand(to_end, hot) * xs.astype(F32)).astype(BF16)
        carry[:, s] = mm(b_t, weighted) + expand(keep_rows, hot)[0:1, :] * carry[:, s]
        y = mm(c_mat, entering[:, s]) * expand(reach, hot) + expand(skip_rows, hot)[0:1, :] * x
        top = y[:half]
        low = y[half:]
        pair = xs_s[:, s]
        per = LANES // width
        for q in range(per):
            head = c * per + q
            masked = jnp.where(lane // width == q, pair, jnp.zeros_like(pair))
            cum_row = cum_t[head : head + 1, :]
            diff = cum_s[:half, head : head + 1] - cum_row[:, :half]
            w = (jnp.exp2(jnp.minimum(diff, 0.0)) * gram[:half, :half]).astype(BF16)
            top = top + mm(w, masked[:half])
            diff = cum_s[half:, head : head + 1] - cum_row
            w = (jnp.exp2(jnp.minimum(diff, 0.0)) * gram[half:, :]).astype(BF16)
            low = low + mm(w, masked)
        y_o[:half, s] = top
        y_o[half:, s] = low
    for c in range(tiles):
        s = slice(c * LANES, (c + 1) * LANES)
        gate = gate_o[:, s]
        gated = y_o[:, s] * (gate * jax.nn.sigmoid(gate))
        d_gn = mm(cot[...], out_w[s, :], NT) * valid
        dgn_o[:, s] = d_gn
        square = square + gated * gated
        dotted = dotted + gated * (d_gn * gng[:, s])
    sums_o[...] = jnp.concatenate(
        [jnp.sum(square.T, axis=0, keepdims=True), jnp.sum(dotted.T, axis=0, keepdims=True)], axis=0
    )
    ubuf[0:8, :] = ubuf[group : group + 8, :]
    vbuf[0:8, :] = vbuf[group : group + 8, :]
    segbuf[0:8, :] = segbuf[group : group + 8, :]


def gate_kernel(dims, sums, seg_row, y_i, gate_i, dgn_i, gng, gn_o, dy_o, dgate_o, ggn_o):
    group, channels, inner = dims

    @pl.when(pl.program_id(0) == 0)
    def _():
        ggn_o[...] = jnp.zeros_like(ggn_o)

    def column(v):
        return jnp.broadcast_to(v, (LANES, group)).T

    valid = (column(seg_row[...]) >= 0.0).astype(F32)
    inverse = lax.rsqrt(column(sums[0:1, :]) / inner + EPS)
    pull = inverse * inverse * inverse * (column(sums[1:2, :]) / inner)
    inverse_v = inverse * valid
    for c in range(channels // LANES):
        s = slice(c * LANES, (c + 1) * LANES)
        y = y_i[:, s]
        gate = gate_i[:, s]
        d_gn = dgn_i[:, s]
        sig = jax.nn.sigmoid(gate)
        act = gate * sig
        gated = y * act
        gn_o[:, s] = (gated * inverse_v * gng[:, s]).astype(BF16)
        ggn_o[0:1, s] += jnp.sum(d_gn * gated * inverse, axis=0, keepdims=True)
        d_gated = inverse * (d_gn * gng[:, s]) - gated * pull
        dy_o[:, s] = (d_gated * act).astype(BF16)
        dgate_o[:, s] = (d_gated * y * sig * (1.0 + gate * (1.0 - sig))).astype(BF16)


def backward_kernel(
    dims, *refs
):
    group, channels, base, width, state, blocks, extra = dims
    seg_s, seg_row, dy_i, y_i, z_i, u_i, st_i, step_i, sin_i, conv_w, head_row = refs[:11]
    dinput_o, dstep_o, dstates_o, gconv_o, gcb_o, ghead_o = refs[11 + extra : 17 + extra]
    dzbuf, segbuf, carry, sdot, cum_t, cum_s, gram_t, dgram_t, w_mat, e_mat, s_mat = refs[17 + extra :]
    at = pl.program_id(0)
    block = blocks - 1 - at
    tiles = channels // LANES
    half = group // 2
    last_seg, prev_seg = block_segments(seg_s, block, group)

    @pl.when(at == 0)
    def _():
        dzbuf[group:, :] = jnp.zeros((8, channels), F32)
        segbuf[group:, :] = jnp.full((8, LANES), -5.0, F32)
        carry[...] = jnp.zeros_like(carry)
        sdot[...] = jnp.zeros_like(sdot)
        gconv_o[...] = jnp.zeros_like(gconv_o)
        gcb_o[...] = jnp.zeros_like(gcb_o)
        ghead_o[...] = jnp.zeros_like(ghead_o)

    seg_mat = jnp.broadcast_to(seg_row[...], (group, group))
    seg_full = seg_mat.T
    seg_col = seg_full[:, :LANES]
    segbuf[:group, :] = seg_col
    raw, step, cum, reach, to_end, keep = step_terms(
        step_i[...], seg_col, head_row[...], last_seg, prev_seg, group
    )
    cum_s[...] = cum
    cum_t[...] = cum.T
    onehot = head_onehot(channels, width, base)
    b_mat = st_i[:, :state]
    c_mat = st_i[:, state:]
    row = lax.broadcasted_iota(jnp.int32, (group, group), 0)
    col = lax.broadcasted_iota(jnp.int32, (group, group), 1)
    gram_t[...] = jnp.where((seg_full == seg_mat) & (row <= col), mm(b_mat, c_mat, NT), 0.0)
    dgram_t[...] = jnp.zeros_like(dgram_t)
    c_t = c_mat.T
    leaving = carry[...].astype(BF16)
    lane = lax.broadcasted_iota(jnp.int32, (group, LANES), 1)
    keep_rows = jnp.broadcast_to(keep, (8, LANES))
    skip_rows = jnp.broadcast_to(head_row[2:3, :], (8, LANES))
    masks = [(segbuf[k : k + group, :] == seg_col).astype(F32) for k in range(1, 4)]
    hs_step = jnp.zeros((group, LANES), F32)
    hs_row = jnp.zeros((group, LANES), F32)
    hs_skip = jnp.zeros((8, LANES), F32)
    hs_dot = jnp.zeros((8, LANES), F32)
    per = LANES // width
    for c in range(tiles):
        s = slice(c * LANES, (c + 1) * LANES)
        hot = onehot[:, s]
        z = z_i[:, s]
        sig = jax.nn.sigmoid(z)
        x = (z * sig).astype(BF16).astype(F32)
        step_x = expand(step, hot)
        pair = (step_x * x).astype(BF16)
        d_pair = dy_i[:, s]
        end_x = expand(to_end, hot)
        weighted = (end_x * pair.astype(F32)).astype(BF16)
        w_mat[:, s] = weighted
        from_next = mm(b_mat, leaving[:, s])
        top = jnp.zeros((half, LANES), F32)
        low = jnp.zeros((half, LANES), F32)
        for q in range(per):
            head = base + c * per + q
            pick = lane // width == q
            d_mask = jnp.where(pick, d_pair, jnp.zeros_like(d_pair))
            x_mask = jnp.where(pick, pair, jnp.zeros_like(pair))
            cum_row = cum_t[head : head + 1, :]
            decay = jnp.exp2(jnp.minimum(cum_row - cum_s[:half, head : head + 1], 0.0))
            top = top + mm((decay * gram_t[:half, :]).astype(BF16), d_mask)
            dgram_t[:half, :] += decay * mm(x_mask[:half], d_pair, NT)
            decay = jnp.exp2(jnp.minimum(cum_row[:, half:] - cum_s[half:, head : head + 1], 0.0))
            low = low + mm((decay * gram_t[half:, half:]).astype(BF16), d_mask[half:])
            dgram_t[half:, half:] += decay * mm(x_mask[half:], d_pair[half:], NT)
        d_inner = jnp.concatenate([top, low], axis=0)
        d_xs = d_inner + from_next * end_x
        d_y = d_pair.astype(F32)
        skip_x = expand(skip_rows, hot)[0:1, :]
        reach_x = expand(reach, hot)
        reached = (reach_x * d_y).astype(BF16)
        e_mat[:, s] = reached
        entering = sin_i[:, s]
        s_mat[:, s] = entering.astype(BF16)
        carried = mm(c_mat, s_mat[:, s])
        hs_step = hs_step + head_sum(d_xs * x, hot)
        hs_row = hs_row + head_sum(
            d_y * (y_i[:, s] - skip_x * x - reach_x * carried)
            + reached.astype(F32) * carried
            - d_inner * pair.astype(F32)
            - from_next * weighted.astype(F32),
            hot,
        )
        skip_col = jnp.sum(d_y * x, axis=0, keepdims=True)
        hs_skip = hs_skip + head_sum(jnp.broadcast_to(skip_col, (8, LANES)), hot)
        d_z = (step_x * d_xs + skip_x * d_y) * (sig * (1.0 + z * (1.0 - sig)))
        dzbuf[:group, s] = d_z
        u = u_i[:, s].astype(F32)
        gcb_o[0:1, s] += jnp.sum(d_z, axis=0, keepdims=True)
        gconv_o[0:1, s] += jnp.sum(d_z * u, axis=0, keepdims=True)
        d_u = conv_w[0:1, s] * d_z
        for k in range(1, 4):
            moved = dzbuf[k : k + group, s] * masks[k - 1]
            d_u = d_u + conv_w[k : k + 1, s] * moved
            gconv_o[k : k + 1, s] += jnp.sum(moved * u, axis=0, keepdims=True)
        dinput_o[:, s] = d_u.astype(BF16)
        new = mm(c_t, reached) + expand(keep_rows, hot)[0:1, :] * carry[:, s]
        carry[:, s] = new
        dot_col = jnp.sum(
            new.astype(BF16).astype(F32) * entering, axis=0, keepdims=True
        )
        hs_dot = hs_dot + head_sum(jnp.broadcast_to(dot_col, (8, LANES)), hot)
    d_gram_t = jnp.where((seg_full == seg_mat) & (row <= col), dgram_t[...], 0.0).astype(BF16)
    dstates_o[:, :state] = (mm(d_gram_t, c_mat) + mm(w_mat[...], leaving, NT)).astype(BF16)
    dstates_o[:, state:] = (
        mm(d_gram_t, b_mat, TN) + mm(e_mat[...], s_mat[...], NT)
    ).astype(BF16)

    final = lax.broadcasted_iota(jnp.int32, (group, LANES), 0) == group - 1
    d_cum = hs_row + jnp.where(final, sdot[0:1, :], 0.0)
    upper = (row <= col).astype(F32).astype(BF16)
    d_rate = sum(mm(upper, part) for part in thirds(d_cum))
    neg_a = head_row[3:4, :]
    d_step = (hs_step + neg_a * d_rate) * jax.nn.sigmoid(raw)
    dstep_o[...] = d_step.astype(BF16)
    ghead_o[0:1, :] += jnp.sum(d_step, axis=0, keepdims=True)
    ghead_o[1:2, :] += jnp.sum(d_rate * step, axis=0, keepdims=True) * neg_a
    ghead_o[2:3, :] += hs_skip[0:1, :]
    sdot[...] = hs_dot
    dzbuf[group:, :] = dzbuf[0:8, :]
    segbuf[group:, :] = segbuf[0:8, :]


def state_kernel(dims, place, seg_row, own, got, z_i, u_i, conv_w, dsp_o, gconv_o, gcb_o, dzbuf, segbuf):
    group, channels, blocks = dims
    at = pl.program_id(0)

    @pl.when(at == 0)
    def _():
        dzbuf[group:, :] = jnp.zeros((8, channels), F32)
        segbuf[group:, :] = jnp.full((8, LANES), -5.0, F32)
        gconv_o[...] = jnp.zeros_like(gconv_o)
        gcb_o[...] = jnp.zeros_like(gcb_o)

    seg_col = jnp.broadcast_to(seg_row[...], (LANES, group)).T
    segbuf[:group, :] = seg_col
    masks = [(segbuf[k : k + group, :] == seg_col).astype(F32) for k in range(1, 4)]
    mine = (blocks - 1 - at) // (blocks // 2) == place[0]
    for c in range(channels // LANES):
        s = slice(c * LANES, (c + 1) * LANES)
        z = z_i[:, s]
        sig = jax.nn.sigmoid(z)
        d_z = jnp.where(mine, own[:, s].astype(F32), got[:, s].astype(F32)) * (sig * (1.0 + z * (1.0 - sig)))
        dzbuf[:group, s] = d_z
        u = u_i[:, s]
        gcb_o[0:1, s] += jnp.sum(d_z, axis=0, keepdims=True)
        gconv_o[0:1, s] += jnp.sum(d_z * u, axis=0, keepdims=True)
        d_u = conv_w[0:1, s] * d_z
        for k in range(1, 4):
            moved = dzbuf[k : k + group, s] * masks[k - 1]
            d_u = d_u + conv_w[k : k + 1, s] * moved
            gconv_o[k : k + 1, s] += jnp.sum(moved * u, axis=0, keepdims=True)
        dsp_o[:, s] = d_u.astype(BF16)
    dzbuf[group:, :] = dzbuf[0:8, :]
    segbuf[group:, :] = segbuf[0:8, :]


def project_kernel(dg, di, ds, gate_w, input_w, step_w, *refs):
    total = mm(dg[...], gate_w[...], NT) + mm(di[...], input_w[...], NT)
    refs[-1][...] = (total + mm(ds[...], step_w[...], NT)).astype(BF16)


def final_kernel(half, place, own, got, sb_i, sw, hid, cot, norm_gain, gh_o, gn_o):
    @pl.when(pl.program_id(0) == 0)
    def _():
        gn_o[...] = jnp.zeros_like(gn_o)

    h = hid[...].astype(F32)
    inverse = lax.rsqrt(jnp.mean(h * h, axis=1, keepdims=True) + EPS)
    first = pl.program_id(0) < half
    summed = jnp.where(first, own[...].astype(F32), got[...].astype(F32))
    d_normed = summed + mm(sb_i[...], sw[...], NT)
    hi = h * inverse
    gn_o[0:1, :] += jnp.sum(d_normed * hi, axis=0, keepdims=True)
    scaled = d_normed * norm_gain[...]
    pull = jnp.mean(hi * scaled, axis=1, keepdims=True)
    gh_o[...] = cot[...].astype(F32) + inverse * (scaled - hi * pull)


def bits_of(size):
    return max(size.bit_length() - 1, 0)


def partner(x, axis, size, mask):
    return lax.ppermute(x, axis, [(i, i ^ mask) for i in range(size)])


def small_cost(us):
    return pl.CostEstimate(flops=0, transcendentals=0, bytes_accessed=int(us * 3.3e6))


def spread_kernel(count, place, keep, got, *refs):
    outs = refs[-count:]
    rows = outs[0].shape[0]
    for d in range(count):
        at = pl.multiple_of(place[1 + d] * rows, rows)
        outs[d][...] = (
            keep[pl.ds(at, rows), :].astype(F32) + got[pl.ds(at, rows), :].astype(F32)
        ).astype(BF16)


def spread_blocks_kernel(count, place, keep, got, *refs):
    outs = refs[-count:]
    for d in range(count):

        @pl.when(pl.program_id(0) == d)
        def _(d=d):
            outs[d][...] = (keep[...].astype(F32) + got[...].astype(F32)).astype(BF16)


def join_kernel(count, place, mine, got, out):
    rows = out.shape[0] // count

    def fill(source):
        for d in range(count):
            at = pl.multiple_of(place[1 + d] * rows, rows)
            out[pl.ds(at, rows), :] = source[d * rows : (d + 1) * rows, :].astype(out.dtype)

    @pl.when(pl.program_id(0) == 0)
    def _():
        fill(mine)

    @pl.when(pl.program_id(0) == 1)
    def _():
        fill(got)


def join_blocks_kernel(count, place, mine, got, out):
    @pl.when(pl.program_id(0) < count)
    def _():
        out[...] = mine[...].astype(F32)

    @pl.when(pl.program_id(0) >= count)
    def _():
        out[...] = got[...].astype(F32)


def start_reduce(x, axis, size):
    near = lax.axis_index(axis) & 1
    rows = x.shape[0] // 2
    send = lax.dynamic_slice_in_dim(x, (1 - near) * rows, rows, 0)
    return x, send, partner(send, axis, size, 1)


def near_reduce(started, axis, size, after=()):
    x, _, got = started
    me = lax.axis_index(axis)
    near, far = me & 1, me >> 1
    count = size // 2
    rows, cols = x.shape[0] // size, x.shape[1]
    order = jnp.stack([far ^ d for d in range(count)])
    outs = [jax.ShapeDtypeStruct((rows, cols), BF16)] * count
    out_spec = pl.BlockSpec((rows, cols), lambda i, pr: (0, 0))
    waits = [pl.BlockSpec(memory_space=pl.ANY)] * len(after)
    if rows % 16 == 0:
        place = jnp.concatenate([near[None], order]).astype(jnp.int32)
        return pl.pallas_call(
            partial(spread_kernel, count),
            name="spread_rows",
            cost_estimate=small_cost(3),
            out_shape=outs,
            grid_spec=pltpu.PrefetchScalarGridSpec(
                num_scalar_prefetch=1,
                grid=(1,),
                in_specs=[
                    pl.BlockSpec((rows * count, cols), lambda i, pr: (pr[0], 0)),
                    pl.BlockSpec((rows * count, cols), lambda i, pr: (0, 0)),
                ] + waits,
                out_specs=[out_spec] * count,
            ),
        )(place, x, got, *after)
    place = jnp.concatenate([near * count + order, order]).astype(jnp.int32)
    return pl.pallas_call(
        partial(spread_blocks_kernel, count),
        name="spread_rows",
        cost_estimate=small_cost(3),
        out_shape=outs,
        grid_spec=pltpu.PrefetchScalarGridSpec(
            num_scalar_prefetch=1,
            grid=(count,),
            in_specs=[
                pl.BlockSpec((rows, cols), lambda i, pr: (pr[i], 0)),
                pl.BlockSpec((rows, cols), lambda i, pr: (pr[count + i], 0)),
            ] + waits,
            out_specs=[out_spec] * count,
        ),
    )(place, x, got, *after)


def add_kernel(count, *refs):
    total = refs[0][...].astype(F32)
    for d in range(1, count):
        total = total + refs[d][...].astype(F32)
    refs[-1][...] = total.astype(BF16)


def far_reduce(parts, axis, size, after=()):
    count = size // 2
    got = [parts[0]] + [partner(parts[d], axis, size, d << 1) for d in range(1, count)]
    spec = pl.BlockSpec(parts[0].shape, lambda: (0, 0))
    return pl.pallas_call(
        partial(add_kernel, count),
        name="add_rows",
        cost_estimate=small_cost(2),
        out_shape=jax.ShapeDtypeStruct(parts[0].shape, BF16),
        in_specs=[spec] * count + [pl.BlockSpec(memory_space=pl.ANY)] * len(after),
        out_specs=spec,
    )(*got, *after)


def gather_rows(x, axis, size):
    me = lax.axis_index(axis)
    near, far = me & 1, me >> 1
    count = size // 2
    rows, cols = x.shape
    mine = jnp.concatenate([x] + [partner(x, axis, size, d << 1) for d in range(1, count)], axis=0)
    got = partner(mine, axis, size, 1)
    order = jnp.stack([far ^ d for d in range(count)])
    if rows % 16 == 0:
        place = jnp.concatenate([near[None], order]).astype(jnp.int32)
        half = pl.BlockSpec((rows * count, cols), lambda i, pr: (0, 0))
        return pl.pallas_call(
            partial(join_kernel, count),
            name="join_rows",
            cost_estimate=small_cost(4),
            out_shape=jax.ShapeDtypeStruct((rows * size, cols), F32),
            grid_spec=pltpu.PrefetchScalarGridSpec(
                num_scalar_prefetch=1,
                grid=(2,),
                in_specs=[half, half],
                out_specs=pl.BlockSpec(
                    (rows * count, cols), lambda i, pr: (jnp.where(i == 0, pr[0], 1 - pr[0]), 0)
                ),
            ),
        )(place, mine, got)
    place = jnp.concatenate([near * count + order, (1 - near) * count + order])
    return pl.pallas_call(
        partial(join_blocks_kernel, count),
        name="join_rows",
        cost_estimate=small_cost(4),
        out_shape=jax.ShapeDtypeStruct((rows * size, cols), F32),
        grid_spec=pltpu.PrefetchScalarGridSpec(
            num_scalar_prefetch=1,
            grid=(size,),
            in_specs=[
                pl.BlockSpec((rows, cols), lambda i, pr: (jnp.minimum(i, count - 1), 0)),
                pl.BlockSpec((rows, cols), lambda i, pr: (jnp.maximum(i - count, 0), 0)),
            ],
            out_specs=pl.BlockSpec((rows, cols), lambda i, pr: (pr[i], 0)),
        ),
    )(place.astype(jnp.int32), mine, got)


def sum_doubling(x, axis, size):
    for b in range(bits_of(size)):
        x = x + partner(x, axis, size, 1 << b)
    return x


def start_half(x, axis, size):
    mine = lax.axis_index(axis) & 1
    half = x.shape[0] // 2
    send = lax.dynamic_slice_in_dim(x, (1 - mine) * half, half, 0)
    return x, partner(send, axis, size, 1)


def near_half(started, axis, size):
    x, got = started
    mine = lax.axis_index(axis) & 1
    keep = lax.dynamic_slice_in_dim(x, mine * got.shape[0], got.shape[0], 0)
    low = (keep.astype(F32) + got.astype(F32)).astype(BF16)
    if bits_of(size) < 2:
        return None, low, None
    return size, low, partner(low, axis, size, 2)


def far_half(state, axis, size):
    _, low, got = state
    total = low.astype(F32)
    if got is not None:
        total = total + got.astype(F32)
    for b in range(2, bits_of(size)):
        low = total.astype(BF16)
        total = low.astype(F32) + partner(low, axis, size, 1 << b).astype(F32)
    return total


def share_half(x, axis, size):
    return x, partner(x, axis, size, 1)


def paste_kernel(place, own, got, out):
    @pl.when(pl.program_id(0) == place[0])
    def _():
        out[...] = own[...]

    @pl.when(pl.program_id(0) != place[0])
    def _():
        out[...] = got[...]


def paste_halves(own, got, me):
    rows, cols = own.shape
    half = pl.BlockSpec((rows, cols), lambda i, pr: (0, 0))
    return pl.pallas_call(
        paste_kernel,
        name="paste_halves",
        cost_estimate=small_cost(4),
        out_shape=jax.ShapeDtypeStruct((rows * 2, cols), own.dtype),
        grid_spec=pltpu.PrefetchScalarGridSpec(
            num_scalar_prefetch=1,
            grid=(2,),
            in_specs=[half, half],
            out_specs=pl.BlockSpec((rows, cols), lambda i, pr: (i, 0)),
        ),
    )((me & 1).astype(jnp.int32).reshape(1), own, got)


def body(
    dp, tensor,
    hidden, segment_ids, norm_gain, gate_weight, input_weight, step_weight, state_weight,
    conv_weight, state_conv_weight, conv_bias, state_conv_bias, step_bias, decay_log,
    skip_gain, gate_norm_gain, out_weight, cotangent,
):
    tokens, model = hidden.shape
    channels = gate_weight.shape[1]
    heads = step_bias.shape[0]
    width = channels // heads
    state = state_weight.shape[1] // 2
    group = GROUP
    blocks = tokens // group
    me_t = lax.axis_index("tensor")
    side = (me_t & 1).astype(jnp.int32).reshape(1)

    seg_row = segment_ids.astype(F32).reshape(blocks, 1, group)
    pad = LANES - heads
    step_w = jnp.pad(step_weight, ((0, 0), (0, pad)))
    neg_a = -jnp.exp(decay_log)
    head_row = jnp.pad(
        jnp.stack([step_bias, neg_a * LOG2E, skip_gain, neg_a]), ((0, 4), (0, pad))
    )
    row2 = lambda v: v.reshape(1, -1)

    full = lambda shape: pl.BlockSpec(shape, lambda i, *_: (0,) * len(shape))
    once = lambda shape: pl.BlockSpec(
        shape, lambda i, *_: (0,) * len(shape), pipeline_mode=pl.Buffered(1)
    )
    tok = lambda cols: pl.BlockSpec((group, cols), lambda i, *_: (i, 0))
    segs = pl.BlockSpec((None, 1, group), lambda i, *_: (i, 0, 0))
    rev = lambda cols: pl.BlockSpec((group, cols), lambda i, *_: (blocks - 1 - i, 0))
    seg_rev = pl.BlockSpec((None, 1, group), lambda i, *_: (blocks - 1 - i, 0, 0))
    sds = jax.ShapeDtypeStruct
    cost = lambda us: pl.CostEstimate(
        flops=0, transcendentals=0, bytes_accessed=int(us * 3.3e6)
    )
    params = pltpu.CompilerParams(
        dimension_semantics=("arbitrary",), vmem_limit_bytes=60 * 1024 * 1024
    )

    (normed, gate_pre, u, z, state_z, state_u, states, step_pre, y, s_in, d_gn, sums) = pl.pallas_call(
        partial(forward_kernel, (group, channels, heads, width, state)),
        name="forward_scan",
        cost_estimate=cost(40),
        out_shape=(
            sds((tokens, model), BF16),
            sds((tokens, channels), F32),
            sds((tokens, channels), BF16),
            sds((tokens, channels), F32),
            sds((tokens, 2 * state), F32),
            sds((tokens, 2 * state), F32),
            sds((tokens, 2 * state), BF16),
            sds((tokens, LANES), F32),
            sds((tokens, channels), F32),
            sds((blocks, state, channels), F32),
            sds((tokens, channels), F32),
            sds((blocks, 2, group), F32),
        ),
        grid_spec=pltpu.PrefetchScalarGridSpec(
            num_scalar_prefetch=1,
            grid=(blocks,),
            in_specs=[
                tok(model), segs, tok(model), once((1, model)),
                once((model, channels)), once((model, channels)), once((model, 2 * state)),
                once((model, LANES)), once((4, channels)), once((1, channels)),
                once((4, 2 * state)), once((1, 2 * state)), once((8, LANES)),
                once((1, channels)), once((channels, model)),
            ],
            out_specs=[
                tok(model), tok(channels), tok(channels), tok(channels), tok(2 * state),
                tok(2 * state), tok(2 * state), tok(LANES), tok(channels),
                pl.BlockSpec((None, state, channels), lambda i, *_: (i, 0, 0)),
                tok(channels),
                pl.BlockSpec((None, 2, group), lambda i, *_: (i, 0, 0)),
            ],
            scratch_shapes=[
                pltpu.VMEM((group + 8, channels), F32),
                pltpu.VMEM((group + 8, 2 * state), F32),
                pltpu.VMEM((group + 8, LANES), F32),
                pltpu.VMEM((state, channels), F32),
                pltpu.VMEM((LANES, group), F32),
                pltpu.VMEM((group, LANES), F32),
                pltpu.VMEM((group, group), F32),
                pltpu.VMEM((group, channels), BF16),
            ],
        ),
        compiler_params=params,
    )(
        segment_ids, hidden, seg_row, cotangent, row2(norm_gain), gate_weight, input_weight,
        state_weight, step_w, conv_weight, row2(conv_bias), state_conv_weight,
        row2(state_conv_bias), head_row, row2(gate_norm_gain), out_weight,
    )

    sums = lax.psum(sums, "tensor")
    gnormed, d_y, d_gate, grad_gnorm = pl.pallas_call(
        partial(gate_kernel, (group, channels, float(channels * tensor))),
        name="gating",
        cost_estimate=cost(10),
        out_shape=(
            sds((tokens, channels), BF16), sds((tokens, channels), BF16),
            sds((tokens, channels), BF16), sds((8, channels), F32),
        ),
        grid_spec=pl.GridSpec(
            grid=(blocks,),
            in_specs=[
                pl.BlockSpec((None, 2, group), lambda i: (i, 0, 0)), segs,
                tok(channels), tok(channels), tok(channels), full((1, channels)),
            ],
            out_specs=[tok(channels), tok(channels), tok(channels), full((8, channels))],
        ),
        compiler_params=params,
    )(sums, seg_row, y, gate_pre, d_gn, row2(gate_norm_gain))

    g_out = start_reduce(mm(gnormed, cotangent, TN).astype(BF16), "dp", dp)
    mix = start_half(mm(gnormed, out_weight).astype(BF16), "tensor", tensor)
    g_gate = start_reduce(mm(normed, d_gate, TN).astype(BF16), "dp", dp)

    part = channels

    def backward(k, waits):
        revc = pl.BlockSpec((group, part), lambda i, *_: (blocks - 1 - i, k))
        return pl.pallas_call(
            partial(
                backward_kernel,
                (group, part, k * (heads // 2), width, state, blocks, len(waits)),
            ),
            name="backward_scan",
            cost_estimate=cost(42),
            out_shape=(
                sds((tokens, part), BF16), sds((tokens, LANES), BF16),
                sds((tokens, 2 * state), BF16), sds((8, part), F32),
                sds((8, part), F32), sds((8, LANES), F32),
            ),
            grid_spec=pltpu.PrefetchScalarGridSpec(
                num_scalar_prefetch=1,
                grid=(blocks,),
                in_specs=[
                    seg_rev, revc, revc, revc, revc, rev(2 * state), rev(LANES),
                    pl.BlockSpec((None, state, part), lambda i, *_: (blocks - 1 - i, 0, k)),
                    pl.BlockSpec((4, part), lambda i, *_: (0, k)), once((8, LANES)),
                ] + [pl.BlockSpec(memory_space=pl.ANY)] * len(waits),
                out_specs=[
                    rev(part), rev(LANES), rev(2 * state),
                    full((8, part)), full((8, part)), full((8, LANES)),
                ],
                scratch_shapes=[
                    pltpu.VMEM((group + 8, part), F32),
                    pltpu.VMEM((group + 8, LANES), F32),
                    pltpu.VMEM((state, part), F32),
                    pltpu.VMEM((8, LANES), F32),
                    pltpu.VMEM((LANES, group), F32),
                    pltpu.VMEM((group, LANES), F32),
                    pltpu.VMEM((group, group), F32),
                    pltpu.VMEM((group, group), F32),
                    pltpu.VMEM((group, part), BF16),
                    pltpu.VMEM((group, part), BF16),
                    pltpu.VMEM((state, part), BF16),
                ],
            ),
            compiler_params=params,
        )(
            segment_ids, seg_row, d_y, y, z, u, states, step_pre, s_in, conv_weight, head_row,
            *waits,
        )

    mix = near_half(mix, "tensor", tensor)
    d_input, d_step, d_states, grad_conv, grad_cb, grad_head = backward(
        0, [g_out[1], mix[1], g_gate[1]]
    )

    states_half = far_half(
        near_half(start_half(d_states, "tensor", tensor), "tensor", tensor), "tensor", tensor,
    ).astype(BF16)
    g_in = start_reduce(mm(normed, d_input, TN).astype(BF16), "dp", dp)
    g_out = near_reduce(g_out, "dp", dp, [d_step])
    g_gate = near_reduce(g_gate, "dp", dp, [d_step])
    local_back = pl.pallas_call(
        project_kernel,
        name="project_back",
        cost_estimate=cost(10),
        out_shape=sds((tokens, model), BF16),
        grid_spec=pl.GridSpec(
            grid=(blocks,),
            in_specs=[
                tok(channels), tok(channels), tok(LANES),
                once((model, channels)), once((model, channels)), once((model, LANES)),
            ] + [pl.BlockSpec(memory_space=pl.ANY)] * 3,
            out_specs=tok(model),
        ),
        compiler_params=params,
    )(
        d_gate, d_input, d_step, gate_weight, input_weight, step_w,
        g_in[1], g_gate[1], g_out[1],
    )
    back_half = near_half(start_half(local_back, "tensor", tensor), "tensor", tensor)
    mix_half = far_half(mix, "tensor", tensor)
    d_states = share_half(states_half, "tensor", tensor)
    low = back_half[1]
    g_out = far_reduce(g_out, "dp", dp, [low])
    g_gate = far_reduce(g_gate, "dp", dp, [low])
    g_in = near_reduce(g_in, "dp", dp, [low])
    g_in = far_reduce(g_in, "dp", dp)
    back_half = far_half(back_half, "tensor", tensor).astype(BF16)

    state_b, grad_sconv, grad_scb = pl.pallas_call(
        partial(state_kernel, (group, 2 * state, blocks)),
        name="state_conv",
        cost_estimate=cost(6),
        out_shape=(
            sds((tokens, 2 * state), BF16), sds((8, 2 * state), F32), sds((8, 2 * state), F32),
        ),
        grid_spec=pltpu.PrefetchScalarGridSpec(
            num_scalar_prefetch=1,
            grid=(blocks,),
            in_specs=[
                seg_rev,
                pl.BlockSpec((group, 2 * state), lambda i, *_: (lax.rem(blocks - 1 - i, blocks // 2), 0)),
                pl.BlockSpec((group, 2 * state), lambda i, *_: (lax.rem(blocks - 1 - i, blocks // 2), 0)),
                rev(2 * state), rev(2 * state), full((4, 2 * state)),
            ],
            out_specs=[rev(2 * state), full((8, 2 * state)), full((8, 2 * state))],
            scratch_shapes=[
                pltpu.VMEM((group + 8, 2 * state), F32), pltpu.VMEM((group + 8, LANES), F32),
            ],
        ),
        compiler_params=params,
    )(side, seg_row, *d_states, state_z, state_u, state_conv_weight)

    rows_t = model // tensor
    normed_part = lax.dynamic_slice_in_dim(normed, me_t * rows_t, rows_t, 1)
    g_state = sum_doubling(mm(normed_part, state_b, TN), "dp", dp).astype(BF16)
    grad_step = mm(d_step, normed, TN)[:16]

    rows = tokens // 2
    hid_half = lax.dynamic_slice_in_dim(hidden, (me_t & 1) * rows, rows, 0)
    out_half = (hid_half.astype(F32) + mix_half).astype(BF16)
    block_out = paste_halves(*share_half(out_half, "tensor", tensor), me_t)
    back = share_half(back_half, "tensor", tensor)

    own_first = lambda cols: pl.BlockSpec(
        (group, cols), lambda i, pr: (lax.rem(i + pr[0] * (blocks // 2), blocks), 0)
    )
    grad_hidden, grad_norm = pl.pallas_call(
        partial(final_kernel, blocks // 2),
        name="final_grad",
        cost_estimate=cost(12),
        out_shape=(sds((tokens, model), F32), sds((8, model), F32)),
        grid_spec=pltpu.PrefetchScalarGridSpec(
            num_scalar_prefetch=1,
            grid=(blocks,),
            in_specs=[
                pl.BlockSpec((group, model), lambda i, pr: (jnp.minimum(i, blocks // 2 - 1), 0)),
                pl.BlockSpec((group, model), lambda i, pr: (jnp.maximum(i - blocks // 2, 0), 0)),
                own_first(2 * state), full((model, 2 * state)), own_first(model),
                own_first(model), full((1, model)),
            ],
            out_specs=[own_first(model), full((8, model))],
        ),
        compiler_params=params,
    )(side, *back, state_b, state_weight, hidden, cotangent, row2(norm_gain))

    grad_out = gather_rows(g_out, "dp", dp)
    grad_gate = gather_rows(g_gate, "dp", dp)
    grad_input = gather_rows(g_in, "dp", dp)
    pieces = [g_state]
    for b in range(bits_of(tensor)):
        low = (me_t >> b) & 1
        pieces = [
            jnp.where(low == 0, jnp.concatenate([v, w]), jnp.concatenate([w, v]))
            for v, w in ((v, partner(v, "tensor", tensor, 1 << b)) for v in pieces)
        ]
    grad_state = pieces[0].astype(F32)

    def line(*parts):
        flat = jnp.concatenate([v.reshape(1, -1) for v in parts], axis=1)
        fill = -flat.shape[1] % model
        return jnp.pad(flat, ((0, 0), (0, fill))).reshape(-1, model)

    taps = conv_weight.shape[0]
    small = jnp.concatenate(
        [
            grad_step,
            grad_norm[0:1],
            line(grad_conv[:taps]),
            line(grad_cb[0:1], grad_gnorm[0:1]),
            line(grad_sconv[:taps], grad_scb[0:1]),
            line(grad_head[0:3]),
        ],
        axis=0,
    )
    fill = -small.shape[0] % 8
    small = sum_doubling(jnp.pad(small, ((0, fill), (0, 0))), "dp", dp)
    flat = small.reshape(-1)
    at = 0

    def take(count, shape):
        nonlocal at
        out = flat[at : at + count].reshape(shape)
        at += count
        return out

    def align():
        nonlocal at
        at += -at % model

    grad_step = small[:heads].T
    at = 16 * model
    grad_norm = take(model, (model,))
    grad_conv = take(taps * channels, (taps, channels))
    align()
    grad_cb = take(channels, (channels,))
    grad_gnorm = take(channels, (channels,))
    align()
    grad_sconv = take(taps * 2 * state, (taps, 2 * state))
    grad_scb = take(2 * state, (2 * state,))
    align()
    heads_out = take(3 * LANES, (3, LANES))
    grad_sbias, grad_decay, grad_skip = (heads_out[k, :heads] for k in range(3))
    return (
        block_out, grad_hidden, grad_norm, grad_gate, grad_input, grad_step, grad_state,
        grad_conv, grad_sconv, grad_cb, grad_scb, grad_sbias, grad_decay, grad_skip,
        grad_gnorm, grad_out,
    )


def solution(mesh):
    return jax.shard_map(
        partial(body, mesh.shape["dp"], mesh.shape["tensor"]),
        mesh=mesh,
        in_specs=(
            P("dp", None), P("dp"), P(), P(None, "tensor"), P(None, "tensor"),
            P(None, "tensor"), P(), P(None, "tensor"), P(), P("tensor"), P(), P("tensor"),
            P("tensor"), P("tensor"), P("tensor"), P("tensor", None), P("dp", None),
        ),
        out_specs=(
            P("dp", None), P("dp", None), P(), P(None, "tensor"), P(None, "tensor"),
            P(None, "tensor"), P(), P(None, "tensor"), P(), P("tensor"), P(), P("tensor"),
            P("tensor"), P("tensor"), P("tensor"), P("tensor", None),
        ),
        check_vma=False,
    )
```

```python
from functools import partial

import jax
import jax.numpy as jnp
from jax import lax
from jax.experimental import pallas as pl
from jax.experimental.pallas import tpu as pltpu
from jax.sharding import PartitionSpec as P


GROUP = 256
LANES = 128
EPS = 1e-05
LOG2E = 1.4426950408889634
F32 = jnp.float32
BF16 = jnp.bfloat16

NN = (((1,), (0,)), ((), ()))
NT = (((1,), (1,)), ((), ()))
TN = (((0,), (0,)), ((), ()))


def mm(left, right, dims=NN):
    return lax.dot_general(left, right, dims, preferred_element_type=F32)


def halves(v):
    high = v.astype(BF16)
    return high, (v - high.astype(F32)).astype(BF16)


def thirds(v):
    high = v.astype(BF16)
    rest = v - high.astype(F32)
    mid = rest.astype(BF16)
    return high, mid, (rest - mid.astype(F32)).astype(BF16)


def expand(v, onehot):
    return mm(jnp.concatenate(halves(v), axis=1), jnp.concatenate([onehot, onehot], axis=0))


def head_sum(v, onehot):
    return mm(jnp.concatenate(halves(v), axis=1), jnp.concatenate([onehot, onehot], axis=1), NT)


def head_onehot(channels, width, base=0):
    lane = lax.broadcasted_iota(jnp.int32, (LANES, channels), 0)
    chan = lax.broadcasted_iota(jnp.int32, (LANES, channels), 1)
    return (lane == base + chan // width).astype(F32).astype(BF16)


def step_terms(step_pre, seg_col, head_row, last_seg, prev_seg, group):
    raw = step_pre + head_row[0:1, :]
    step = jnp.maximum(raw, 0.0) + jnp.log1p(jnp.exp(-jnp.abs(raw)))
    rate2 = step * head_row[1:2, :]
    row = lax.broadcasted_iota(jnp.int32, (group, group), 0)
    col = lax.broadcasted_iota(jnp.int32, (group, group), 1)
    lower = (row >= col).astype(F32).astype(BF16)
    cum = sum(mm(lower, part) for part in thirds(rate2))
    last = cum[group - 1 : group, :]
    reach = jnp.where(seg_col == prev_seg, jnp.exp2(cum), 0.0)
    to_end = jnp.where(seg_col == last_seg, jnp.exp2(jnp.minimum(last - cum, 0.0)), 0.0)
    keep = jnp.exp2(last) * (last_seg == prev_seg).astype(F32)
    return raw, step, cum, reach, to_end, keep


def block_segments(seg_s, block, group):
    last = seg_s[block * group + group - 1].astype(F32)
    prev_at = jnp.maximum(block * group - 1, 0)
    prev = jnp.where(block > 0, seg_s[prev_at].astype(F32), -3.0)
    return last, prev


def forward_kernel(
    dims,
    seg_s, hid, seg_row, cot, norm_gain, gate_w, input_w, state_w, step_w,
    conv_w, conv_b, sconv_w, sconv_b, head_row, gng, out_w,
    normed_o, gate_o, u_o, z_o, sz_o, su_o, st_o, step_o, y_o, sin_o, dgn_o, sums_o,
    ubuf, vbuf, segbuf, carry, cum_t, cum_s, gram, xs_s,
):
    group, channels, _, width, state = dims
    block = pl.program_id(0)
    tiles = channels // LANES
    last_seg, prev_seg = block_segments(seg_s, block, group)

    @pl.when(block == 0)
    def _():
        ubuf[0:8, :] = jnp.zeros((8, channels), F32)
        vbuf[0:8, :] = jnp.zeros((8, 2 * state), F32)
        segbuf[0:8, :] = jnp.full((8, LANES), -2.0, F32)
        carry[...] = jnp.zeros_like(carry)

    h = hid[...].astype(F32)
    inverse = lax.rsqrt(jnp.mean(h * h, axis=1, keepdims=True) + EPS)
    normed = (h * inverse * norm_gain[...]).astype(BF16)
    normed_o[...] = normed
    step_pre = mm(normed, step_w[...])
    step_o[...] = step_pre
    ubuf[8:, :] = mm(normed, input_w[...])
    vbuf[8:, :] = mm(normed, state_w[...])
    gate_o[...] = mm(normed, gate_w[...])
    dgn_o[...] = mm(cot[...], out_w[...], NT)

    seg_mat = jnp.broadcast_to(seg_row[...], (group, group))
    seg_full = seg_mat.T
    seg_col = seg_full[:, :LANES]
    segbuf[8:, :] = seg_col
    valid = (seg_col >= 0.0).astype(F32)
    same = [(segbuf[8 - k : 8 - k + group, :] == seg_col).astype(F32) for k in range(1, 4)]

    _, step, cum, reach, to_end, keep = step_terms(
        step_pre, seg_col, head_row[...], last_seg, prev_seg, group
    )
    cum_s[...] = cum
    cum_t[...] = cum.T
    onehot = head_onehot(channels, width)

    for c in range(2 * state // LANES):
        s = slice(c * LANES, (c + 1) * LANES)
        z = sconv_b[:, s] + sconv_w[0:1, s] * vbuf[8:, s]
        for k in range(1, 4):
            z = z + sconv_w[k : k + 1, s] * (vbuf[8 - k : 8 - k + group, s] * same[k - 1])
        sz_o[:, s] = z
        su_o[:, s] = vbuf[8:, s]
        st_o[:, s] = (z * jax.nn.sigmoid(z)).astype(BF16)
    b_mat = st_o[:, :state]
    c_mat = st_o[:, state:]

    row = lax.broadcasted_iota(jnp.int32, (group, group), 0)
    col = lax.broadcasted_iota(jnp.int32, (group, group), 1)
    gram[...] = jnp.where((seg_full == seg_mat) & (row >= col), mm(c_mat, b_mat, NT), 0.0)

    sin_o[...] = carry[...]
    entering = carry[...].astype(BF16)
    b_t = b_mat.T
    lane = lax.broadcasted_iota(jnp.int32, (group, LANES), 1)
    half = group // 2
    square = jnp.zeros((group, LANES), F32)
    dotted = jnp.zeros((group, LANES), F32)
    keep_rows = jnp.broadcast_to(keep, (8, LANES))
    skip_rows = jnp.broadcast_to(head_row[2:3, :], (8, LANES))
    for c in range(tiles):
        s = slice(c * LANES, (c + 1) * LANES)
        hot = onehot[:, s]
        z = conv_b[:, s] + conv_w[0:1, s] * ubuf[8:, s]
        for k in range(1, 4):
            z = z + conv_w[k : k + 1, s] * (ubuf[8 - k : 8 - k + group, s] * same[k - 1])
        z_o[:, s] = z
        u_o[:, s] = ubuf[8:, s].astype(BF16)
        x = (z * jax.nn.sigmoid(z)).astype(BF16).astype(F32)
        xs = (expand(step, hot) * x).astype(BF16)
        xs_s[:, s] = xs
        weighted = (expand(to_end, hot) * xs.astype(F32)).astype(BF16)
        carry[:, s] = mm(b_t, weighted) + expand(keep_rows, hot)[0:1, :] * carry[:, s]
        y = mm(c_mat, entering[:, s]) * expand(reach, hot) + expand(skip_rows, hot)[0:1, :] * x
        top = y[:half]
        low = y[half:]
        pair = xs_s[:, s]
        per = LANES // width
        upper_w, upper_x = [], []
        for q in range(per):
            head = c * per + q
            masked = jnp.where(lane // width == q, pair, jnp.zeros_like(pair))
            cum_row = cum_t[head : head + 1, :]
            diff = cum_s[:half, head : head + 1] - cum_row[:, :half]
            w = (jnp.exp2(jnp.minimum(diff, 0.0)) * gram[:half, :half]).astype(BF16)
            upper_w.append(w)
            upper_x.append(masked[:half])
            diff = cum_s[half:, head : head + 1] - cum_row
            w = (jnp.exp2(jnp.minimum(diff, 0.0)) * gram[half:, :]).astype(BF16)
            low = low + mm(w, masked)
        top = top + mm(jnp.concatenate(upper_w, axis=1), jnp.concatenate(upper_x, axis=0))
        y_o[:half, s] = top
        y_o[half:, s] = low
    for c in range(tiles):
        s = slice(c * LANES, (c + 1) * LANES)
        gate = gate_o[:, s]
        gated = y_o[:, s] * (gate * jax.nn.sigmoid(gate))
        d_gn = dgn_o[:, s] * valid
        dgn_o[:, s] = d_gn
        square = square + gated * gated
        dotted = dotted + gated * (d_gn * gng[:, s])
    sums_o[...] = jnp.concatenate(
        [jnp.sum(square.T, axis=0, keepdims=True), jnp.sum(dotted.T, axis=0, keepdims=True)], axis=0
    )
    ubuf[0:8, :] = ubuf[group : group + 8, :]
    vbuf[0:8, :] = vbuf[group : group + 8, :]
    segbuf[0:8, :] = segbuf[group : group + 8, :]


def gate_kernel(dims, sums, seg_row, y_i, gate_i, dgn_i, gng, gn_o, dy_o, dgate_o, ggn_o):
    group, channels, inner = dims

    @pl.when(pl.program_id(0) == 0)
    def _():
        ggn_o[...] = jnp.zeros_like(ggn_o)

    def column(v):
        return jnp.broadcast_to(v, (LANES, group)).T

    valid = (column(seg_row[...]) >= 0.0).astype(F32)
    inverse = lax.rsqrt(column(sums[0:1, :]) / inner + EPS)
    pull = inverse * inverse * inverse * (column(sums[1:2, :]) / inner)
    inverse_v = inverse * valid
    for c in range(channels // LANES):
        s = slice(c * LANES, (c + 1) * LANES)
        y = y_i[:, s]
        gate = gate_i[:, s]
        d_gn = dgn_i[:, s]
        sig = jax.nn.sigmoid(gate)
        act = gate * sig
        gated = y * act
        gn_o[:, s] = (gated * inverse_v * gng[:, s]).astype(BF16)
        ggn_o[0:1, s] += jnp.sum(d_gn * gated * inverse, axis=0, keepdims=True)
        d_gated = inverse * (d_gn * gng[:, s]) - gated * pull
        dy_o[:, s] = (d_gated * act).astype(BF16)
        dgate_o[:, s] = (d_gated * y * sig * (1.0 + gate * (1.0 - sig))).astype(BF16)


def backward_kernel(
    dims, *refs
):
    group, channels, base, width, state, blocks, extra = dims
    seg_s, seg_row, dy_i, y_i, z_i, u_i, st_i, step_i, sin_i, conv_w, head_row = refs[:11]
    dinput_o, dstep_o, dstates_o, gconv_o, gcb_o, ghead_o = refs[11 + extra : 17 + extra]
    dzbuf, segbuf, carry, sdot, cum_t, cum_s, gram_t, dgram_t, w_mat, e_mat, s_mat = refs[17 + extra :]
    at = pl.program_id(0)
    block = blocks - 1 - at
    tiles = channels // LANES
    half = group // 2
    last_seg, prev_seg = block_segments(seg_s, block, group)

    @pl.when(at == 0)
    def _():
        dzbuf[group:, :] = jnp.zeros((8, channels), F32)
        segbuf[group:, :] = jnp.full((8, LANES), -5.0, F32)
        carry[...] = jnp.zeros_like(carry)
        sdot[...] = jnp.zeros_like(sdot)
        gconv_o[...] = jnp.zeros_like(gconv_o)
        gcb_o[...] = jnp.zeros_like(gcb_o)
        ghead_o[...] = jnp.zeros_like(ghead_o)

    seg_mat = jnp.broadcast_to(seg_row[...], (group, group))
    seg_full = seg_mat.T
    seg_col = seg_full[:, :LANES]
    segbuf[:group, :] = seg_col
    raw, step, cum, reach, to_end, keep = step_terms(
        step_i[...], seg_col, head_row[...], last_seg, prev_seg, group
    )
    cum_s[...] = cum
    cum_t[...] = cum.T
    onehot = head_onehot(channels, width, base)
    b_mat = st_i[:, :state]
    c_mat = st_i[:, state:]
    row = lax.broadcasted_iota(jnp.int32, (group, group), 0)
    col = lax.broadcasted_iota(jnp.int32, (group, group), 1)
    gram_t[...] = jnp.where((seg_full == seg_mat) & (row <= col), mm(b_mat, c_mat, NT), 0.0)
    dgram_t[...] = jnp.zeros_like(dgram_t)
    c_t = c_mat.T
    leaving = carry[...].astype(BF16)
    lane = lax.broadcasted_iota(jnp.int32, (group, LANES), 1)
    keep_rows = jnp.broadcast_to(keep, (8, LANES))
    skip_rows = jnp.broadcast_to(head_row[2:3, :], (8, LANES))
    masks = [(segbuf[k : k + group, :] == seg_col).astype(F32) for k in range(1, 4)]
    hs_step = jnp.zeros((group, LANES), F32)
    hs_row = jnp.zeros((group, LANES), F32)
    hs_skip = jnp.zeros((8, LANES), F32)
    hs_dot = jnp.zeros((8, LANES), F32)
    per = LANES // width
    for c in range(tiles):
        s = slice(c * LANES, (c + 1) * LANES)
        hot = onehot[:, s]
        z = z_i[:, s]
        sig = jax.nn.sigmoid(z)
        x = (z * sig).astype(BF16).astype(F32)
        step_x = expand(step, hot)
        pair = (step_x * x).astype(BF16)
        d_pair = dy_i[:, s]
        end_x = expand(to_end, hot)
        weighted = (end_x * pair.astype(F32)).astype(BF16)
        w_mat[:, s] = weighted
        from_next = mm(b_mat, leaving[:, s])
        top = jnp.zeros((half, LANES), F32)
        lower_w, lower_d = [], []
        for q in range(per):
            head = base + c * per + q
            pick = lane // width == q
            d_mask = jnp.where(pick, d_pair, jnp.zeros_like(d_pair))
            x_mask = jnp.where(pick, pair, jnp.zeros_like(pair))
            cum_row = cum_t[head : head + 1, :]
            decay = jnp.exp2(jnp.minimum(cum_row - cum_s[:half, head : head + 1], 0.0))
            top = top + mm((decay * gram_t[:half, :]).astype(BF16), d_mask)
            dgram_t[:half, :] += decay * mm(x_mask[:half], d_pair, NT)
            decay = jnp.exp2(jnp.minimum(cum_row[:, half:] - cum_s[half:, head : head + 1], 0.0))
            lower_w.append((decay * gram_t[half:, half:]).astype(BF16))
            lower_d.append(d_mask[half:])
            dgram_t[half:, half:] += decay * mm(x_mask[half:], d_pair[half:], NT)
        low = mm(jnp.concatenate(lower_w, axis=1), jnp.concatenate(lower_d, axis=0))
        d_inner = jnp.concatenate([top, low], axis=0)
        d_xs = d_inner + from_next * end_x
        d_y = d_pair.astype(F32)
        skip_x = expand(skip_rows, hot)[0:1, :]
        reach_x = expand(reach, hot)
        reached = (reach_x * d_y).astype(BF16)
        e_mat[:, s] = reached
        entering = sin_i[:, s]
        s_mat[:, s] = entering.astype(BF16)
        carried = mm(c_mat, s_mat[:, s])
        hs_step = hs_step + head_sum(d_xs * x, hot)
        hs_row = hs_row + head_sum(
            d_y * (y_i[:, s] - skip_x * x - reach_x * carried)
            + reached.astype(F32) * carried
            - d_inner * pair.astype(F32)
            - from_next * weighted.astype(F32),
            hot,
        )
        skip_col = jnp.sum(d_y * x, axis=0, keepdims=True)
        hs_skip = hs_skip + head_sum(jnp.broadcast_to(skip_col, (8, LANES)), hot)
        d_z = (step_x * d_xs + skip_x * d_y) * (sig * (1.0 + z * (1.0 - sig)))
        dzbuf[:group, s] = d_z
        u = u_i[:, s].astype(F32)
        gcb_o[0:1, s] += jnp.sum(d_z, axis=0, keepdims=True)
        gconv_o[0:1, s] += jnp.sum(d_z * u, axis=0, keepdims=True)
        d_u = conv_w[0:1, s] * d_z
        for k in range(1, 4):
            moved = dzbuf[k : k + group, s] * masks[k - 1]
            d_u = d_u + conv_w[k : k + 1, s] * moved
            gconv_o[k : k + 1, s] += jnp.sum(moved * u, axis=0, keepdims=True)
        dinput_o[:, s] = d_u.astype(BF16)
        new = mm(c_t, reached) + expand(keep_rows, hot)[0:1, :] * carry[:, s]
        carry[:, s] = new
        dot_col = jnp.sum(
            new.astype(BF16).astype(F32) * entering, axis=0, keepdims=True
        )
        hs_dot = hs_dot + head_sum(jnp.broadcast_to(dot_col, (8, LANES)), hot)
    d_gram_t = jnp.where((seg_full == seg_mat) & (row <= col), dgram_t[...], 0.0).astype(BF16)
    dstates_o[:, :state] = (mm(d_gram_t, c_mat) + mm(w_mat[...], leaving, NT)).astype(BF16)
    dstates_o[:, state:] = (
        mm(d_gram_t, b_mat, TN) + mm(e_mat[...], s_mat[...], NT)
    ).astype(BF16)

    final = lax.broadcasted_iota(jnp.int32, (group, LANES), 0) == group - 1
    d_cum = hs_row + jnp.where(final, sdot[0:1, :], 0.0)
    upper = (row <= col).astype(F32).astype(BF16)
    d_rate = sum(mm(upper, part) for part in thirds(d_cum))
    neg_a = head_row[3:4, :]
    d_step = (hs_step + neg_a * d_rate) * jax.nn.sigmoid(raw)
    dstep_o[...] = d_step.astype(BF16)
    ghead_o[0:1, :] += jnp.sum(d_step, axis=0, keepdims=True)
    ghead_o[1:2, :] += jnp.sum(d_rate * step, axis=0, keepdims=True) * neg_a
    ghead_o[2:3, :] += hs_skip[0:1, :]
    sdot[...] = hs_dot
    dzbuf[group:, :] = dzbuf[0:8, :]
    segbuf[group:, :] = segbuf[0:8, :]


def state_kernel(dims, place, seg_row, own, got, z_i, u_i, conv_w, dsp_o, gconv_o, gcb_o, dzbuf, segbuf):
    group, channels, blocks = dims
    at = pl.program_id(0)

    @pl.when(at == 0)
    def _():
        dzbuf[group:, :] = jnp.zeros((8, channels), F32)
        segbuf[group:, :] = jnp.full((8, LANES), -5.0, F32)
        gconv_o[...] = jnp.zeros_like(gconv_o)
        gcb_o[...] = jnp.zeros_like(gcb_o)

    seg_col = jnp.broadcast_to(seg_row[...], (LANES, group)).T
    segbuf[:group, :] = seg_col
    masks = [(segbuf[k : k + group, :] == seg_col).astype(F32) for k in range(1, 4)]
    mine = (blocks - 1 - at) // (blocks // 2) == place[0]
    for c in range(channels // LANES):
        s = slice(c * LANES, (c + 1) * LANES)
        z = z_i[:, s]
        sig = jax.nn.sigmoid(z)
        d_z = jnp.where(mine, own[:, s].astype(F32), got[:, s].astype(F32)) * (sig * (1.0 + z * (1.0 - sig)))
        dzbuf[:group, s] = d_z
        u = u_i[:, s]
        gcb_o[0:1, s] += jnp.sum(d_z, axis=0, keepdims=True)
        gconv_o[0:1, s] += jnp.sum(d_z * u, axis=0, keepdims=True)
        d_u = conv_w[0:1, s] * d_z
        for k in range(1, 4):
            moved = dzbuf[k : k + group, s] * masks[k - 1]
            d_u = d_u + conv_w[k : k + 1, s] * moved
            gconv_o[k : k + 1, s] += jnp.sum(moved * u, axis=0, keepdims=True)
        dsp_o[:, s] = d_u.astype(BF16)
    dzbuf[group:, :] = dzbuf[0:8, :]
    segbuf[group:, :] = segbuf[0:8, :]


def project_kernel(dg, di, ds, gate_w, input_w, step_w, *refs):
    total = mm(dg[...], gate_w[...], NT) + mm(di[...], input_w[...], NT)
    refs[-1][...] = (total + mm(ds[...], step_w[...], NT)).astype(BF16)


def final_kernel(half, place, own, got, sb_i, sw, hid, cot, norm_gain, gh_o, gn_o):
    @pl.when(pl.program_id(0) == 0)
    def _():
        gn_o[...] = jnp.zeros_like(gn_o)

    h = hid[...].astype(F32)
    inverse = lax.rsqrt(jnp.mean(h * h, axis=1, keepdims=True) + EPS)
    first = pl.program_id(0) < half
    summed = jnp.where(first, own[...].astype(F32), got[...].astype(F32))
    d_normed = summed + mm(sb_i[...], sw[...], NT)
    hi = h * inverse
    gn_o[0:1, :] += jnp.sum(d_normed * hi, axis=0, keepdims=True)
    scaled = d_normed * norm_gain[...]
    pull = jnp.mean(hi * scaled, axis=1, keepdims=True)
    gh_o[...] = cot[...].astype(F32) + inverse * (scaled - hi * pull)


def bits_of(size):
    return max(size.bit_length() - 1, 0)


def partner(x, axis, size, mask):
    return lax.ppermute(x, axis, [(i, i ^ mask) for i in range(size)])


def small_cost(us):
    return pl.CostEstimate(flops=0, transcendentals=0, bytes_accessed=int(us * 3.3e6))


def spread_kernel(count, place, keep, got, *refs):
    outs = refs[-count:]
    rows = outs[0].shape[0]
    for d in range(count):
        at = pl.multiple_of(place[1 + d] * rows, rows)
        outs[d][...] = (
            keep[pl.ds(at, rows), :].astype(F32) + got[pl.ds(at, rows), :].astype(F32)
        ).astype(BF16)


def spread_blocks_kernel(count, place, keep, got, *refs):
    outs = refs[-count:]
    for d in range(count):

        @pl.when(pl.program_id(0) == d)
        def _(d=d):
            outs[d][...] = (keep[...].astype(F32) + got[...].astype(F32)).astype(BF16)


def join_kernel(count, place, mine, got, out):
    rows = out.shape[0] // count

    def fill(source):
        for d in range(count):
            at = pl.multiple_of(place[1 + d] * rows, rows)
            out[pl.ds(at, rows), :] = source[d * rows : (d + 1) * rows, :].astype(out.dtype)

    @pl.when(pl.program_id(0) == 0)
    def _():
        fill(mine)

    @pl.when(pl.program_id(0) == 1)
    def _():
        fill(got)


def join_blocks_kernel(count, place, mine, got, out):
    @pl.when(pl.program_id(0) < count)
    def _():
        out[...] = mine[...].astype(F32)

    @pl.when(pl.program_id(0) >= count)
    def _():
        out[...] = got[...].astype(F32)


def start_reduce(x, axis, size):
    near = lax.axis_index(axis) & 1
    rows = x.shape[0] // 2
    send = lax.dynamic_slice_in_dim(x, (1 - near) * rows, rows, 0)
    return x, send, partner(send, axis, size, 1)


def near_reduce(started, axis, size, after=()):
    x, _, got = started
    me = lax.axis_index(axis)
    near, far = me & 1, me >> 1
    count = size // 2
    rows, cols = x.shape[0] // size, x.shape[1]
    order = jnp.stack([far ^ d for d in range(count)])
    outs = [jax.ShapeDtypeStruct((rows, cols), BF16)] * count
    out_spec = pl.BlockSpec((rows, cols), lambda i, pr: (0, 0))
    waits = [pl.BlockSpec(memory_space=pl.ANY)] * len(after)
    if rows % 16 == 0:
        place = jnp.concatenate([near[None], order]).astype(jnp.int32)
        return pl.pallas_call(
            partial(spread_kernel, count),
            name="spread_rows",
            cost_estimate=small_cost(3),
            out_shape=outs,
            grid_spec=pltpu.PrefetchScalarGridSpec(
                num_scalar_prefetch=1,
                grid=(1,),
                in_specs=[
                    pl.BlockSpec((rows * count, cols), lambda i, pr: (pr[0], 0)),
                    pl.BlockSpec((rows * count, cols), lambda i, pr: (0, 0)),
                ] + waits,
                out_specs=[out_spec] * count,
            ),
        )(place, x, got, *after)
    place = jnp.concatenate([near * count + order, order]).astype(jnp.int32)
    return pl.pallas_call(
        partial(spread_blocks_kernel, count),
        name="spread_rows",
        cost_estimate=small_cost(3),
        out_shape=outs,
        grid_spec=pltpu.PrefetchScalarGridSpec(
            num_scalar_prefetch=1,
            grid=(count,),
            in_specs=[
                pl.BlockSpec((rows, cols), lambda i, pr: (pr[i], 0)),
                pl.BlockSpec((rows, cols), lambda i, pr: (pr[count + i], 0)),
            ] + waits,
            out_specs=[out_spec] * count,
        ),
    )(place, x, got, *after)


def add_kernel(count, *refs):
    total = refs[0][...].astype(F32)
    for d in range(1, count):
        total = total + refs[d][...].astype(F32)
    refs[-1][...] = total.astype(BF16)


def far_reduce(parts, axis, size, after=()):
    count = size // 2
    got = [parts[0]] + [partner(parts[d], axis, size, d << 1) for d in range(1, count)]
    spec = pl.BlockSpec(parts[0].shape, lambda: (0, 0))
    return pl.pallas_call(
        partial(add_kernel, count),
        name="add_rows",
        cost_estimate=small_cost(2),
        out_shape=jax.ShapeDtypeStruct(parts[0].shape, BF16),
        in_specs=[spec] * count + [pl.BlockSpec(memory_space=pl.ANY)] * len(after),
        out_specs=spec,
    )(*got, *after)


def gather_rows(x, axis, size):
    me = lax.axis_index(axis)
    near, far = me & 1, me >> 1
    count = size // 2
    rows, cols = x.shape
    mine = jnp.concatenate([x] + [partner(x, axis, size, d << 1) for d in range(1, count)], axis=0)
    got = partner(mine, axis, size, 1)
    order = jnp.stack([far ^ d for d in range(count)])
    if rows % 16 == 0:
        place = jnp.concatenate([near[None], order]).astype(jnp.int32)
        half = pl.BlockSpec((rows * count, cols), lambda i, pr: (0, 0))
        return pl.pallas_call(
            partial(join_kernel, count),
            name="join_rows",
            cost_estimate=small_cost(4),
            out_shape=jax.ShapeDtypeStruct((rows * size, cols), F32),
            grid_spec=pltpu.PrefetchScalarGridSpec(
                num_scalar_prefetch=1,
                grid=(2,),
                in_specs=[half, half],
                out_specs=pl.BlockSpec(
                    (rows * count, cols), lambda i, pr: (jnp.where(i == 0, pr[0], 1 - pr[0]), 0)
                ),
            ),
        )(place, mine, got)
    place = jnp.concatenate([near * count + order, (1 - near) * count + order])
    return pl.pallas_call(
        partial(join_blocks_kernel, count),
        name="join_rows",
        cost_estimate=small_cost(4),
        out_shape=jax.ShapeDtypeStruct((rows * size, cols), F32),
        grid_spec=pltpu.PrefetchScalarGridSpec(
            num_scalar_prefetch=1,
            grid=(size,),
            in_specs=[
                pl.BlockSpec((rows, cols), lambda i, pr: (jnp.minimum(i, count - 1), 0)),
                pl.BlockSpec((rows, cols), lambda i, pr: (jnp.maximum(i - count, 0), 0)),
            ],
            out_specs=pl.BlockSpec((rows, cols), lambda i, pr: (pr[i], 0)),
        ),
    )(place.astype(jnp.int32), mine, got)


def sum_doubling(x, axis, size, hop=F32):
    for b in range(bits_of(size)):
        low = x.astype(hop)
        x = low.astype(F32) + partner(low, axis, size, 1 << b).astype(F32)
    return x


def start_half(x, axis, size):
    mine = lax.axis_index(axis) & 1
    half = x.shape[0] // 2
    send = lax.dynamic_slice_in_dim(x, (1 - mine) * half, half, 0)
    return x, partner(send, axis, size, 1)


def near_half(started, axis, size):
    x, got = started
    mine = lax.axis_index(axis) & 1
    keep = lax.dynamic_slice_in_dim(x, mine * got.shape[0], got.shape[0], 0)
    low = (keep.astype(F32) + got.astype(F32)).astype(BF16)
    if bits_of(size) < 2:
        return None, low, None
    return size, low, partner(low, axis, size, 2)


def far_half(state, axis, size):
    _, low, got = state
    total = low.astype(F32)
    if got is not None:
        total = total + got.astype(F32)
    for b in range(2, bits_of(size)):
        low = total.astype(BF16)
        total = low.astype(F32) + partner(low, axis, size, 1 << b).astype(F32)
    return total


def share_half(x, axis, size):
    return x, partner(x, axis, size, 1)


def paste_kernel(place, own, got, out):
    @pl.when(pl.program_id(0) == place[0])
    def _():
        out[...] = own[...]

    @pl.when(pl.program_id(0) != place[0])
    def _():
        out[...] = got[...]


def paste_halves(own, got, me):
    rows, cols = own.shape
    half = pl.BlockSpec((rows, cols), lambda i, pr: (0, 0))
    return pl.pallas_call(
        paste_kernel,
        name="paste_halves",
        cost_estimate=small_cost(4),
        out_shape=jax.ShapeDtypeStruct((rows * 2, cols), own.dtype),
        grid_spec=pltpu.PrefetchScalarGridSpec(
            num_scalar_prefetch=1,
            grid=(2,),
            in_specs=[half, half],
            out_specs=pl.BlockSpec((rows, cols), lambda i, pr: (i, 0)),
        ),
    )((me & 1).astype(jnp.int32).reshape(1), own, got)


def body(
    dp, tensor,
    hidden, segment_ids, norm_gain, gate_weight, input_weight, step_weight, state_weight,
    conv_weight, state_conv_weight, conv_bias, state_conv_bias, step_bias, decay_log,
    skip_gain, gate_norm_gain, out_weight, cotangent,
):
    tokens, model = hidden.shape
    channels = gate_weight.shape[1]
    heads = step_bias.shape[0]
    width = channels // heads
    state = state_weight.shape[1] // 2
    group = GROUP
    blocks = tokens // group
    me_t = lax.axis_index("tensor")
    side = (me_t & 1).astype(jnp.int32).reshape(1)

    seg_row = segment_ids.astype(F32).reshape(blocks, 1, group)
    pad = LANES - heads
    step_w = jnp.pad(step_weight, ((0, 0), (0, pad)))
    neg_a = -jnp.exp(decay_log)
    head_row = jnp.pad(
        jnp.stack([step_bias, neg_a * LOG2E, skip_gain, neg_a]), ((0, 4), (0, pad))
    )
    row2 = lambda v: v.reshape(1, -1)

    full = lambda shape: pl.BlockSpec(shape, lambda i, *_: (0,) * len(shape))
    once = lambda shape: pl.BlockSpec(
        shape, lambda i, *_: (0,) * len(shape), pipeline_mode=pl.Buffered(1)
    )
    tok = lambda cols: pl.BlockSpec((group, cols), lambda i, *_: (i, 0))
    segs = pl.BlockSpec((None, 1, group), lambda i, *_: (i, 0, 0))
    rev = lambda cols: pl.BlockSpec((group, cols), lambda i, *_: (blocks - 1 - i, 0))
    seg_rev = pl.BlockSpec((None, 1, group), lambda i, *_: (blocks - 1 - i, 0, 0))
    sds = jax.ShapeDtypeStruct
    cost = lambda us: pl.CostEstimate(
        flops=0, transcendentals=0, bytes_accessed=int(us * 3.3e6)
    )
    params = pltpu.CompilerParams(
        dimension_semantics=("arbitrary",), vmem_limit_bytes=60 * 1024 * 1024
    )

    (normed, gate_pre, u, z, state_z, state_u, states, step_pre, y, s_in, d_gn, sums) = pl.pallas_call(
        partial(forward_kernel, (group, channels, heads, width, state)),
        name="forward_scan",
        cost_estimate=cost(40),
        out_shape=(
            sds((tokens, model), BF16),
            sds((tokens, channels), F32),
            sds((tokens, channels), BF16),
            sds((tokens, channels), F32),
            sds((tokens, 2 * state), F32),
            sds((tokens, 2 * state), F32),
            sds((tokens, 2 * state), BF16),
            sds((tokens, LANES), F32),
            sds((tokens, channels), F32),
            sds((blocks, state, channels), F32),
            sds((tokens, channels), F32),
            sds((blocks, 2, group), F32),
        ),
        grid_spec=pltpu.PrefetchScalarGridSpec(
            num_scalar_prefetch=1,
            grid=(blocks,),
            in_specs=[
                tok(model), segs, tok(model), once((1, model)),
                once((model, channels)), once((model, channels)), once((model, 2 * state)),
                once((model, LANES)), once((4, channels)), once((1, channels)),
                once((4, 2 * state)), once((1, 2 * state)), once((8, LANES)),
                once((1, channels)), once((channels, model)),
            ],
            out_specs=[
                tok(model), tok(channels), tok(channels), tok(channels), tok(2 * state),
                tok(2 * state), tok(2 * state), tok(LANES), tok(channels),
                pl.BlockSpec((None, state, channels), lambda i, *_: (i, 0, 0)),
                tok(channels),
                pl.BlockSpec((None, 2, group), lambda i, *_: (i, 0, 0)),
            ],
            scratch_shapes=[
                pltpu.VMEM((group + 8, channels), F32),
                pltpu.VMEM((group + 8, 2 * state), F32),
                pltpu.VMEM((group + 8, LANES), F32),
                pltpu.VMEM((state, channels), F32),
                pltpu.VMEM((LANES, group), F32),
                pltpu.VMEM((group, LANES), F32),
                pltpu.VMEM((group, group), F32),
                pltpu.VMEM((group, channels), BF16),
            ],
        ),
        compiler_params=params,
    )(
        segment_ids, hidden, seg_row, cotangent, row2(norm_gain), gate_weight, input_weight,
        state_weight, step_w, conv_weight, row2(conv_bias), state_conv_weight,
        row2(state_conv_bias), head_row, row2(gate_norm_gain), out_weight,
    )

    sums = sum_doubling(sums, "tensor", tensor)
    gnormed, d_y, d_gate, grad_gnorm = pl.pallas_call(
        partial(gate_kernel, (group, channels, float(channels * tensor))),
        name="gating",
        cost_estimate=cost(10),
        out_shape=(
            sds((tokens, channels), BF16), sds((tokens, channels), BF16),
            sds((tokens, channels), BF16), sds((8, channels), F32),
        ),
        grid_spec=pl.GridSpec(
            grid=(blocks,),
            in_specs=[
                pl.BlockSpec((None, 2, group), lambda i: (i, 0, 0)), segs,
                tok(channels), tok(channels), tok(channels), full((1, channels)),
            ],
            out_specs=[tok(channels), tok(channels), tok(channels), full((8, channels))],
        ),
        compiler_params=params,
    )(sums, seg_row, y, gate_pre, d_gn, row2(gate_norm_gain))

    g_out = start_reduce(mm(gnormed, cotangent, TN).astype(BF16), "dp", dp)
    mix = mm(gnormed, out_weight).astype(BF16)
    mix = start_half(mix, "tensor", tensor)
    g_gate = mm(normed, d_gate, TN).astype(BF16)
    g_gate = start_reduce(g_gate, "dp", dp)

    part = channels

    def backward(k, waits):
        revc = pl.BlockSpec((group, part), lambda i, *_: (blocks - 1 - i, k))
        return pl.pallas_call(
            partial(
                backward_kernel,
                (group, part, k * (heads // 2), width, state, blocks, len(waits)),
            ),
            name="backward_scan",
            cost_estimate=cost(42),
            out_shape=(
                sds((tokens, part), BF16), sds((tokens, LANES), BF16),
                sds((tokens, 2 * state), BF16), sds((8, part), F32),
                sds((8, part), F32), sds((8, LANES), F32),
            ),
            grid_spec=pltpu.PrefetchScalarGridSpec(
                num_scalar_prefetch=1,
                grid=(blocks,),
                in_specs=[
                    seg_rev, revc, revc, revc, revc, rev(2 * state), rev(LANES),
                    pl.BlockSpec((None, state, part), lambda i, *_: (blocks - 1 - i, 0, k)),
                    pl.BlockSpec((4, part), lambda i, *_: (0, k)), once((8, LANES)),
                ] + [pl.BlockSpec(memory_space=pl.ANY)] * len(waits),
                out_specs=[
                    rev(part), rev(LANES), rev(2 * state),
                    full((8, part)), full((8, part)), full((8, LANES)),
                ],
                scratch_shapes=[
                    pltpu.VMEM((group + 8, part), F32),
                    pltpu.VMEM((group + 8, LANES), F32),
                    pltpu.VMEM((state, part), F32),
                    pltpu.VMEM((8, LANES), F32),
                    pltpu.VMEM((LANES, group), F32),
                    pltpu.VMEM((group, LANES), F32),
                    pltpu.VMEM((group, group), F32),
                    pltpu.VMEM((group, group), F32),
                    pltpu.VMEM((group, part), BF16),
                    pltpu.VMEM((group, part), BF16),
                    pltpu.VMEM((state, part), BF16),
                ],
            ),
            compiler_params=params,
        )(
            segment_ids, seg_row, d_y, y, z, u, states, step_pre, s_in, conv_weight, head_row,
            *waits,
        )

    mix = near_half(mix, "tensor", tensor)
    g_out = near_reduce(g_out, "dp", dp, [mix[1], g_gate[1]])
    d_input, d_step, d_states, grad_conv, grad_cb, grad_head = backward(
        0, [g_out[1]]
    )

    states_half = far_half(
        near_half(start_half(d_states, "tensor", tensor), "tensor", tensor), "tensor", tensor,
    ).astype(BF16)
    g_in = start_reduce(mm(normed, d_input, TN).astype(BF16), "dp", dp)
    g_out = far_reduce(g_out, "dp", dp, [d_step])
    g_gate = near_reduce(g_gate, "dp", dp, [d_step])
    local_back = pl.pallas_call(
        project_kernel,
        name="project_back",
        cost_estimate=cost(10),
        out_shape=sds((tokens, model), BF16),
        grid_spec=pl.GridSpec(
            grid=(blocks,),
            in_specs=[
                tok(channels), tok(channels), tok(LANES),
                once((model, channels)), once((model, channels)), once((model, LANES)),
            ] + [pl.BlockSpec(memory_space=pl.ANY)] * 3,
            out_specs=tok(model),
        ),
        compiler_params=params,
    )(
        d_gate, d_input, d_step, gate_weight, input_weight, step_w,
        g_in[1], g_gate[1], g_out,
    )
    back_half = near_half(start_half(local_back, "tensor", tensor), "tensor", tensor)
    mix_half = far_half(mix, "tensor", tensor)
    d_states = share_half(states_half, "tensor", tensor)
    low = back_half[1]
    g_gate = far_reduce(g_gate, "dp", dp, [low])
    g_in = near_reduce(g_in, "dp", dp, [low])
    g_in = far_reduce(g_in, "dp", dp)
    back_half = far_half(back_half, "tensor", tensor).astype(BF16)

    state_b, grad_sconv, grad_scb = pl.pallas_call(
        partial(state_kernel, (group, 2 * state, blocks)),
        name="state_conv",
        cost_estimate=cost(6),
        out_shape=(
            sds((tokens, 2 * state), BF16), sds((8, 2 * state), F32), sds((8, 2 * state), F32),
        ),
        grid_spec=pltpu.PrefetchScalarGridSpec(
            num_scalar_prefetch=1,
            grid=(blocks,),
            in_specs=[
                seg_rev,
                pl.BlockSpec((group, 2 * state), lambda i, *_: (lax.rem(blocks - 1 - i, blocks // 2), 0)),
                pl.BlockSpec((group, 2 * state), lambda i, *_: (lax.rem(blocks - 1 - i, blocks // 2), 0)),
                rev(2 * state), rev(2 * state), full((4, 2 * state)),
            ],
            out_specs=[rev(2 * state), full((8, 2 * state)), full((8, 2 * state))],
            scratch_shapes=[
                pltpu.VMEM((group + 8, 2 * state), F32), pltpu.VMEM((group + 8, LANES), F32),
            ],
        ),
        compiler_params=params,
    )(side, seg_row, *d_states, state_z, state_u, state_conv_weight)

    rows_t = model // tensor
    normed_part = lax.dynamic_slice_in_dim(normed, me_t * rows_t, rows_t, 1)
    g_state = mm(normed_part, state_b, TN)
    grad_step = mm(d_step, normed, TN)[:16]

    rows = tokens // 2
    hid_half = lax.dynamic_slice_in_dim(hidden, (me_t & 1) * rows, rows, 0)
    out_half = (hid_half.astype(F32) + mix_half).astype(BF16)
    block_out = paste_halves(*share_half(out_half, "tensor", tensor), me_t)
    back = share_half(back_half, "tensor", tensor)

    own_first = lambda cols: pl.BlockSpec(
        (group, cols), lambda i, pr: (lax.rem(i + pr[0] * (blocks // 2), blocks), 0)
    )
    grad_hidden, grad_norm = pl.pallas_call(
        partial(final_kernel, blocks // 2),
        name="final_grad",
        cost_estimate=cost(12),
        out_shape=(sds((tokens, model), F32), sds((8, model), F32)),
        grid_spec=pltpu.PrefetchScalarGridSpec(
            num_scalar_prefetch=1,
            grid=(blocks,),
            in_specs=[
                pl.BlockSpec((group, model), lambda i, pr: (jnp.minimum(i, blocks // 2 - 1), 0)),
                pl.BlockSpec((group, model), lambda i, pr: (jnp.maximum(i - blocks // 2, 0), 0)),
                own_first(2 * state), full((model, 2 * state)), own_first(model),
                own_first(model), full((1, model)),
            ],
            out_specs=[own_first(model), full((8, model))],
        ),
        compiler_params=params,
    )(side, *back, state_b, state_weight, hidden, cotangent, row2(norm_gain))

    grad_out = gather_rows(g_out, "dp", dp)
    grad_gate = gather_rows(g_gate, "dp", dp)
    grad_input = gather_rows(g_in, "dp", dp)

    def line(*parts):
        flat = jnp.concatenate([v.reshape(1, -1) for v in parts], axis=1)
        fill = -flat.shape[1] % model
        return jnp.pad(flat, ((0, 0), (0, fill))).reshape(-1, model)

    taps = conv_weight.shape[0]
    small = jnp.concatenate(
        [
            grad_step,
            line(grad_conv[:taps]),
            line(grad_cb[0:1], grad_gnorm[0:1]),
            line(grad_sconv[:taps], grad_scb[0:1]),
            line(grad_head[0:3]),
        ],
        axis=0,
    )
    fill = -small.shape[0] % 8
    small = jnp.pad(small, ((0, fill), (0, 0)))
    lines = small.shape[0]
    small = sum_doubling(
        jnp.concatenate([small, g_state.reshape(-1, model)], axis=0), "dp", dp, BF16
    )
    g_state = small[lines:].reshape(rows_t, 2 * state).astype(BF16)
    grad_norm = sum_doubling(grad_norm, "dp", dp)[0]
    pieces = [g_state]
    for b in range(bits_of(tensor)):
        low = (me_t >> b) & 1
        pieces = [
            jnp.where(low == 0, jnp.concatenate([v, w]), jnp.concatenate([w, v]))
            for v, w in ((v, partner(v, "tensor", tensor, 1 << b)) for v in pieces)
        ]
    grad_state = pieces[0].astype(F32)

    flat = small.reshape(-1)
    at = 0

    def take(count, shape):
        nonlocal at
        out = flat[at : at + count].reshape(shape)
        at += count
        return out

    def align():
        nonlocal at
        at += -at % model

    grad_step = small[:heads].T
    at = 16 * model
    grad_conv = take(taps * channels, (taps, channels))
    align()
    grad_cb = take(channels, (channels,))
    grad_gnorm = take(channels, (channels,))
    align()
    grad_sconv = take(taps * 2 * state, (taps, 2 * state))
    grad_scb = take(2 * state, (2 * state,))
    align()
    heads_out = take(3 * LANES, (3, LANES))
    grad_sbias, grad_decay, grad_skip = (heads_out[k, :heads] for k in range(3))
    return (
        block_out, grad_hidden, grad_norm, grad_gate, grad_input, grad_step, grad_state,
        grad_conv, grad_sconv, grad_cb, grad_scb, grad_sbias, grad_decay, grad_skip,
        grad_gnorm, grad_out,
    )


def solution(mesh):
    return jax.shard_map(
        partial(body, mesh.shape["dp"], mesh.shape["tensor"]),
        mesh=mesh,
        in_specs=(
            P("dp", None), P("dp"), P(), P(None, "tensor"), P(None, "tensor"),
            P(None, "tensor"), P(), P(None, "tensor"), P(), P("tensor"), P(), P("tensor"),
            P("tensor"), P("tensor"), P("tensor"), P("tensor", None), P("dp", None),
        ),
        out_specs=(
            P("dp", None), P("dp", None), P(), P(None, "tensor"), P(None, "tensor"),
            P(None, "tensor"), P(), P(None, "tensor"), P(), P("tensor"), P(), P("tensor"),
            P("tensor"), P("tensor"), P("tensor"), P("tensor", None),
        ),
        check_vma=False,
    )
```

```python
from functools import partial

import jax
import jax.numpy as jnp
from jax import lax
from jax.experimental import pallas as pl
from jax.experimental.pallas import tpu as pltpu
from jax.sharding import PartitionSpec as P


GROUP = 256
LANES = 128
EPS = 1e-05
DP, TENSOR = "dp", "tensor"
LOG2E = 1.4426950408889634
F32 = jnp.float32
BF16 = jnp.bfloat16

NN = (((1,), (0,)), ((), ()))
NT = (((1,), (1,)), ((), ()))
TN = (((0,), (0,)), ((), ()))


def mm(left, right, dims=NN):
    return lax.dot_general(left, right, dims, preferred_element_type=F32)


def halves(v):
    high = v.astype(BF16)
    return high, (v - high.astype(F32)).astype(BF16)


def thirds(v):
    high = v.astype(BF16)
    rest = v - high.astype(F32)
    mid = rest.astype(BF16)
    return high, mid, (rest - mid.astype(F32)).astype(BF16)


def expand(v, onehot):
    return mm(jnp.concatenate(halves(v), axis=1), jnp.concatenate([onehot, onehot], axis=0))


def head_sum(v, onehot):
    return mm(jnp.concatenate(halves(v), axis=1), jnp.concatenate([onehot, onehot], axis=1), NT)


def head_onehot(channels, width, base=0):
    lane = lax.broadcasted_iota(jnp.int32, (LANES, channels), 0)
    chan = lax.broadcasted_iota(jnp.int32, (LANES, channels), 1)
    return (lane == base + chan // width).astype(F32).astype(BF16)


def step_terms(step_pre, seg_col, head_row, last_seg, prev_seg, group):
    raw = step_pre + head_row[0:1, :]
    step = jnp.maximum(raw, 0.0) + jnp.log1p(jnp.exp(-jnp.abs(raw)))
    rate2 = step * head_row[1:2, :]
    row = lax.broadcasted_iota(jnp.int32, (group, group), 0)
    col = lax.broadcasted_iota(jnp.int32, (group, group), 1)
    lower = (row >= col).astype(F32).astype(BF16)
    cum = sum(mm(lower, part) for part in thirds(rate2))
    last = cum[group - 1 : group, :]
    reach = jnp.where(seg_col == prev_seg, jnp.exp2(cum), 0.0)
    to_end = jnp.where(seg_col == last_seg, jnp.exp2(jnp.minimum(last - cum, 0.0)), 0.0)
    keep = jnp.exp2(last) * (last_seg == prev_seg).astype(F32)
    return raw, step, cum, reach, to_end, keep


def block_segments(seg_s, block, group):
    last = seg_s[block * group + group - 1].astype(F32)
    prev_at = jnp.maximum(block * group - 1, 0)
    prev = jnp.where(block > 0, seg_s[prev_at].astype(F32), -3.0)
    return last, prev


def forward_kernel(
    dims,
    seg_s, hid, seg_row, cot, norm_gain, gate_w, input_w, state_w, step_w,
    conv_w, conv_b, sconv_w, sconv_b, head_row, gng, out_w,
    normed_o, gate_o, u_o, z_o, sz_o, su_o, st_o, step_o, y_o, sin_o, dgn_o, sums_o,
    ubuf, vbuf, segbuf, carry, cum_t, cum_s, gram, xs_s,
):
    group, channels, _, width, state = dims
    block = pl.program_id(0)
    tiles = channels // LANES
    last_seg, prev_seg = block_segments(seg_s, block, group)

    @pl.when(block == 0)
    def _():
        ubuf[0:8, :] = jnp.zeros((8, channels), F32)
        vbuf[0:8, :] = jnp.zeros((8, 2 * state), F32)
        segbuf[0:8, :] = jnp.full((8, LANES), -2.0, F32)
        carry[...] = jnp.zeros_like(carry)

    h = hid[...].astype(F32)
    inverse = lax.rsqrt(jnp.mean(h * h, axis=1, keepdims=True) + EPS)
    normed = (h * inverse * norm_gain[...]).astype(BF16)
    normed_o[...] = normed
    step_pre = mm(normed, step_w[...])
    step_o[...] = step_pre
    ubuf[8:, :] = mm(normed, input_w[...])
    vbuf[8:, :] = mm(normed, state_w[...])
    gate_o[...] = mm(normed, gate_w[...])
    dgn_o[...] = mm(cot[...], out_w[...], NT)

    seg_mat = jnp.broadcast_to(seg_row[...], (group, group))
    seg_full = seg_mat.T
    seg_col = seg_full[:, :LANES]
    segbuf[8:, :] = seg_col
    valid = (seg_col >= 0.0).astype(F32)
    same = [(segbuf[8 - k : 8 - k + group, :] == seg_col).astype(F32) for k in range(1, 4)]

    _, step, cum, reach, to_end, keep = step_terms(
        step_pre, seg_col, head_row[...], last_seg, prev_seg, group
    )
    cum_s[...] = cum
    cum_t[...] = cum.T
    onehot = head_onehot(channels, width)

    for c in range(2 * state // LANES):
        s = slice(c * LANES, (c + 1) * LANES)
        z = sconv_b[:, s] + sconv_w[0:1, s] * vbuf[8:, s]
        for k in range(1, 4):
            z = z + sconv_w[k : k + 1, s] * (vbuf[8 - k : 8 - k + group, s] * same[k - 1])
        sz_o[:, s] = z
        su_o[:, s] = vbuf[8:, s]
        st_o[:, s] = (z * jax.nn.sigmoid(z)).astype(BF16)
    b_mat = st_o[:, :state]
    c_mat = st_o[:, state:]

    row = lax.broadcasted_iota(jnp.int32, (group, group), 0)
    col = lax.broadcasted_iota(jnp.int32, (group, group), 1)
    gram[...] = jnp.where((seg_full == seg_mat) & (row >= col), mm(c_mat, b_mat, NT), 0.0)

    sin_o[...] = carry[...]
    entering = carry[...].astype(BF16)
    b_t = b_mat.T
    lane = lax.broadcasted_iota(jnp.int32, (group, LANES), 1)
    half = group // 2
    square = jnp.zeros((group, LANES), F32)
    dotted = jnp.zeros((group, LANES), F32)
    keep_rows = jnp.broadcast_to(keep, (8, LANES))
    skip_rows = jnp.broadcast_to(head_row[2:3, :], (8, LANES))
    for c in range(tiles):
        s = slice(c * LANES, (c + 1) * LANES)
        hot = onehot[:, s]
        z = conv_b[:, s] + conv_w[0:1, s] * ubuf[8:, s]
        for k in range(1, 4):
            z = z + conv_w[k : k + 1, s] * (ubuf[8 - k : 8 - k + group, s] * same[k - 1])
        z_o[:, s] = z
        u_o[:, s] = ubuf[8:, s].astype(BF16)
        x = (z * jax.nn.sigmoid(z)).astype(BF16).astype(F32)
        xs = (expand(step, hot) * x).astype(BF16)
        xs_s[:, s] = xs
        weighted = (expand(to_end, hot) * xs.astype(F32)).astype(BF16)
        carry[:, s] = mm(b_t, weighted) + expand(keep_rows, hot)[0:1, :] * carry[:, s]
        y = mm(c_mat, entering[:, s]) * expand(reach, hot) + expand(skip_rows, hot)[0:1, :] * x
        top = y[:half]
        low = y[half:]
        pair = xs_s[:, s]
        per = LANES // width
        upper_w, upper_x = [], []
        for q in range(per):
            head = c * per + q
            masked = jnp.where(lane // width == q, pair, jnp.zeros_like(pair))
            cum_row = cum_t[head : head + 1, :]
            diff = cum_s[:half, head : head + 1] - cum_row[:, :half]
            w = (jnp.exp2(jnp.minimum(diff, 0.0)) * gram[:half, :half]).astype(BF16)
            upper_w.append(w)
            upper_x.append(masked[:half])
            diff = cum_s[half:, head : head + 1] - cum_row
            w = (jnp.exp2(jnp.minimum(diff, 0.0)) * gram[half:, :]).astype(BF16)
            low = low + mm(w, masked)
        top = top + mm(jnp.concatenate(upper_w, axis=1), jnp.concatenate(upper_x, axis=0))
        y_o[:half, s] = top
        y_o[half:, s] = low
    for c in range(tiles):
        s = slice(c * LANES, (c + 1) * LANES)
        gate = gate_o[:, s]
        gated = y_o[:, s] * (gate * jax.nn.sigmoid(gate))
        d_gn = dgn_o[:, s] * valid
        dgn_o[:, s] = d_gn
        square = square + gated * gated
        dotted = dotted + gated * (d_gn * gng[:, s])
    sums_o[...] = jnp.concatenate(
        [jnp.sum(square.T, axis=0, keepdims=True), jnp.sum(dotted.T, axis=0, keepdims=True)], axis=0
    )
    ubuf[0:8, :] = ubuf[group : group + 8, :]
    vbuf[0:8, :] = vbuf[group : group + 8, :]
    segbuf[0:8, :] = segbuf[group : group + 8, :]


def gate_kernel(dims, sums, seg_row, y_i, gate_i, dgn_i, gng, gn_o, dy_o, dgate_o, ggn_o):
    group, channels, inner = dims

    @pl.when(pl.program_id(0) == 0)
    def _():
        ggn_o[...] = jnp.zeros_like(ggn_o)

    def column(v):
        return jnp.broadcast_to(v, (LANES, group)).T

    valid = (column(seg_row[...]) >= 0.0).astype(F32)
    inverse = lax.rsqrt(column(sums[0:1, :]) / inner + EPS)
    pull = inverse * inverse * inverse * (column(sums[1:2, :]) / inner)
    inverse_v = inverse * valid
    for c in range(channels // LANES):
        s = slice(c * LANES, (c + 1) * LANES)
        y = y_i[:, s]
        gate = gate_i[:, s]
        d_gn = dgn_i[:, s]
        sig = jax.nn.sigmoid(gate)
        act = gate * sig
        gated = y * act
        gn_o[:, s] = (gated * inverse_v * gng[:, s]).astype(BF16)
        ggn_o[0:1, s] += jnp.sum(d_gn * gated * inverse, axis=0, keepdims=True)
        d_gated = inverse * (d_gn * gng[:, s]) - gated * pull
        dy_o[:, s] = (d_gated * act).astype(BF16)
        dgate_o[:, s] = (d_gated * y * sig * (1.0 + gate * (1.0 - sig))).astype(BF16)


def backward_kernel(
    dims, *refs
):
    group, channels, base, width, state, blocks, extra = dims
    seg_s, seg_row, dy_i, y_i, z_i, u_i, st_i, step_i, sin_i, conv_w, head_row = refs[:11]
    dinput_o, dstep_o, dstates_o, gconv_o, gcb_o, ghead_o = refs[11 + extra : 17 + extra]
    dzbuf, segbuf, carry, sdot, cum_t, cum_s, gram_t, dgram_t, w_mat, e_mat, s_mat = refs[17 + extra :]
    at = pl.program_id(0)
    block = blocks - 1 - at
    tiles = channels // LANES
    half = group // 2
    last_seg, prev_seg = block_segments(seg_s, block, group)

    @pl.when(at == 0)
    def _():
        dzbuf[group:, :] = jnp.zeros((8, channels), F32)
        segbuf[group:, :] = jnp.full((8, LANES), -5.0, F32)
        carry[...] = jnp.zeros_like(carry)
        sdot[...] = jnp.zeros_like(sdot)
        gconv_o[...] = jnp.zeros_like(gconv_o)
        gcb_o[...] = jnp.zeros_like(gcb_o)
        ghead_o[...] = jnp.zeros_like(ghead_o)

    seg_mat = jnp.broadcast_to(seg_row[...], (group, group))
    seg_full = seg_mat.T
    seg_col = seg_full[:, :LANES]
    segbuf[:group, :] = seg_col
    raw, step, cum, reach, to_end, keep = step_terms(
        step_i[...], seg_col, head_row[...], last_seg, prev_seg, group
    )
    cum_s[...] = cum
    cum_t[...] = cum.T
    onehot = head_onehot(channels, width, base)
    b_mat = st_i[:, :state]
    c_mat = st_i[:, state:]
    row = lax.broadcasted_iota(jnp.int32, (group, group), 0)
    col = lax.broadcasted_iota(jnp.int32, (group, group), 1)
    gram_t[...] = jnp.where((seg_full == seg_mat) & (row <= col), mm(b_mat, c_mat, NT), 0.0)
    dgram_t[...] = jnp.zeros_like(dgram_t)
    c_t = c_mat.T
    leaving = carry[...].astype(BF16)
    lane = lax.broadcasted_iota(jnp.int32, (group, LANES), 1)
    keep_rows = jnp.broadcast_to(keep, (8, LANES))
    skip_rows = jnp.broadcast_to(head_row[2:3, :], (8, LANES))
    masks = [(segbuf[k : k + group, :] == seg_col).astype(F32) for k in range(1, 4)]
    hs_step = jnp.zeros((group, LANES), F32)
    hs_row = jnp.zeros((group, LANES), F32)
    hs_skip = jnp.zeros((8, LANES), F32)
    hs_dot = jnp.zeros((8, LANES), F32)
    per = LANES // width
    for c in range(tiles):
        s = slice(c * LANES, (c + 1) * LANES)
        hot = onehot[:, s]
        z = z_i[:, s]
        sig = jax.nn.sigmoid(z)
        x = (z * sig).astype(BF16).astype(F32)
        step_x = expand(step, hot)
        pair = (step_x * x).astype(BF16)
        d_pair = dy_i[:, s]
        end_x = expand(to_end, hot)
        weighted = (end_x * pair.astype(F32)).astype(BF16)
        w_mat[:, s] = weighted
        from_next = mm(b_mat, leaving[:, s])
        top = jnp.zeros((half, LANES), F32)
        lower_w, lower_d = [], []
        for q in range(per):
            head = base + c * per + q
            pick = lane // width == q
            d_mask = jnp.where(pick, d_pair, jnp.zeros_like(d_pair))
            x_mask = jnp.where(pick, pair, jnp.zeros_like(pair))
            cum_row = cum_t[head : head + 1, :]
            decay = jnp.exp2(jnp.minimum(cum_row - cum_s[:half, head : head + 1], 0.0))
            top = top + mm((decay * gram_t[:half, :]).astype(BF16), d_mask)
            dgram_t[:half, :] += decay * mm(x_mask[:half], d_pair, NT)
            decay = jnp.exp2(jnp.minimum(cum_row[:, half:] - cum_s[half:, head : head + 1], 0.0))
            lower_w.append((decay * gram_t[half:, half:]).astype(BF16))
            lower_d.append(d_mask[half:])
            dgram_t[half:, half:] += decay * mm(x_mask[half:], d_pair[half:], NT)
        low = mm(jnp.concatenate(lower_w, axis=1), jnp.concatenate(lower_d, axis=0))
        d_inner = jnp.concatenate([top, low], axis=0)
        d_xs = d_inner + from_next * end_x
        d_y = d_pair.astype(F32)
        skip_x = expand(skip_rows, hot)[0:1, :]
        reach_x = expand(reach, hot)
        reached = (reach_x * d_y).astype(BF16)
        e_mat[:, s] = reached
        entering = sin_i[:, s]
        s_mat[:, s] = entering.astype(BF16)
        carried = mm(c_mat, s_mat[:, s])
        hs_step = hs_step + head_sum(d_xs * x, hot)
        hs_row = hs_row + head_sum(
            d_y * (y_i[:, s] - skip_x * x - reach_x * carried)
            + reached.astype(F32) * carried
            - d_inner * pair.astype(F32)
            - from_next * weighted.astype(F32),
            hot,
        )
        skip_col = jnp.sum(d_y * x, axis=0, keepdims=True)
        hs_skip = hs_skip + head_sum(jnp.broadcast_to(skip_col, (8, LANES)), hot)
        d_z = (step_x * d_xs + skip_x * d_y) * (sig * (1.0 + z * (1.0 - sig)))
        dzbuf[:group, s] = d_z
        u = u_i[:, s].astype(F32)
        gcb_o[0:1, s] += jnp.sum(d_z, axis=0, keepdims=True)
        gconv_o[0:1, s] += jnp.sum(d_z * u, axis=0, keepdims=True)
        d_u = conv_w[0:1, s] * d_z
        for k in range(1, 4):
            moved = dzbuf[k : k + group, s] * masks[k - 1]
            d_u = d_u + conv_w[k : k + 1, s] * moved
            gconv_o[k : k + 1, s] += jnp.sum(moved * u, axis=0, keepdims=True)
        dinput_o[:, s] = d_u.astype(BF16)
        new = mm(c_t, reached) + expand(keep_rows, hot)[0:1, :] * carry[:, s]
        carry[:, s] = new
        dot_col = jnp.sum(
            new.astype(BF16).astype(F32) * entering, axis=0, keepdims=True
        )
        hs_dot = hs_dot + head_sum(jnp.broadcast_to(dot_col, (8, LANES)), hot)
    d_gram_t = jnp.where((seg_full == seg_mat) & (row <= col), dgram_t[...], 0.0).astype(BF16)
    dstates_o[:, :state] = (mm(d_gram_t, c_mat) + mm(w_mat[...], leaving, NT)).astype(BF16)
    dstates_o[:, state:] = (
        mm(d_gram_t, b_mat, TN) + mm(e_mat[...], s_mat[...], NT)
    ).astype(BF16)

    final = lax.broadcasted_iota(jnp.int32, (group, LANES), 0) == group - 1
    d_cum = hs_row + jnp.where(final, sdot[0:1, :], 0.0)
    upper = (row <= col).astype(F32).astype(BF16)
    d_rate = sum(mm(upper, part) for part in thirds(d_cum))
    neg_a = head_row[3:4, :]
    d_step = (hs_step + neg_a * d_rate) * jax.nn.sigmoid(raw)
    dstep_o[...] = d_step.astype(BF16)
    ghead_o[0:1, :] += jnp.sum(d_step, axis=0, keepdims=True)
    ghead_o[1:2, :] += jnp.sum(d_rate * step, axis=0, keepdims=True) * neg_a
    ghead_o[2:3, :] += hs_skip[0:1, :]
    sdot[...] = hs_dot
    dzbuf[group:, :] = dzbuf[0:8, :]
    segbuf[group:, :] = segbuf[0:8, :]


def state_kernel(dims, place, seg_row, own, got, z_i, u_i, conv_w, dsp_o, gconv_o, gcb_o, dzbuf, segbuf):
    group, channels, blocks = dims
    at = pl.program_id(0)

    @pl.when(at == 0)
    def _():
        dzbuf[group:, :] = jnp.zeros((8, channels), F32)
        segbuf[group:, :] = jnp.full((8, LANES), -5.0, F32)
        gconv_o[...] = jnp.zeros_like(gconv_o)
        gcb_o[...] = jnp.zeros_like(gcb_o)

    seg_col = jnp.broadcast_to(seg_row[...], (LANES, group)).T
    segbuf[:group, :] = seg_col
    masks = [(segbuf[k : k + group, :] == seg_col).astype(F32) for k in range(1, 4)]
    mine = (blocks - 1 - at) // (blocks // 2) == place[0]
    for c in range(channels // LANES):
        s = slice(c * LANES, (c + 1) * LANES)
        z = z_i[:, s]
        sig = jax.nn.sigmoid(z)
        d_z = jnp.where(mine, own[:, s].astype(F32), got[:, s].astype(F32)) * (sig * (1.0 + z * (1.0 - sig)))
        dzbuf[:group, s] = d_z
        u = u_i[:, s]
        gcb_o[0:1, s] += jnp.sum(d_z, axis=0, keepdims=True)
        gconv_o[0:1, s] += jnp.sum(d_z * u, axis=0, keepdims=True)
        d_u = conv_w[0:1, s] * d_z
        for k in range(1, 4):
            moved = dzbuf[k : k + group, s] * masks[k - 1]
            d_u = d_u + conv_w[k : k + 1, s] * moved
            gconv_o[k : k + 1, s] += jnp.sum(moved * u, axis=0, keepdims=True)
        dsp_o[:, s] = d_u.astype(BF16)
    dzbuf[group:, :] = dzbuf[0:8, :]
    segbuf[group:, :] = segbuf[0:8, :]


def project_kernel(dg, di, ds, gate_w, input_w, step_w, *refs):
    total = mm(dg[...], gate_w[...], NT) + mm(di[...], input_w[...], NT)
    refs[-1][...] = (total + mm(ds[...], step_w[...], NT)).astype(BF16)


def final_kernel(half, place, own, got, sb_i, sw, hid, cot, norm_gain, gh_o, gn_o):
    @pl.when(pl.program_id(0) == 0)
    def _():
        gn_o[...] = jnp.zeros_like(gn_o)

    h = hid[...].astype(F32)
    inverse = lax.rsqrt(jnp.mean(h * h, axis=1, keepdims=True) + EPS)
    first = pl.program_id(0) < half
    summed = jnp.where(first, own[...].astype(F32), got[...].astype(F32))
    d_normed = summed + mm(sb_i[...], sw[...], NT)
    hi = h * inverse
    gn_o[0:1, :] += jnp.sum(d_normed * hi, axis=0, keepdims=True)
    scaled = d_normed * norm_gain[...]
    pull = jnp.mean(hi * scaled, axis=1, keepdims=True)
    gh_o[...] = cot[...].astype(F32) + inverse * (scaled - hi * pull)


def bits_of(size):
    return max(size.bit_length() - 1, 0)


def partner(x, axis, size, mask):
    return lax.ppermute(x, axis, [(i, i ^ mask) for i in range(size)])


def small_cost(us):
    return pl.CostEstimate(flops=0, transcendentals=0, bytes_accessed=int(us * 3.3e6))


def spread_kernel(count, place, keep, got, *refs):
    outs = refs[-count:]
    rows = outs[0].shape[0]
    for d in range(count):
        at = pl.multiple_of(place[1 + d] * rows, rows)
        outs[d][...] = (
            keep[pl.ds(at, rows), :].astype(F32) + got[pl.ds(at, rows), :].astype(F32)
        ).astype(BF16)


def spread_blocks_kernel(count, place, keep, got, *refs):
    outs = refs[-count:]
    for d in range(count):

        @pl.when(pl.program_id(0) == d)
        def _(d=d):
            outs[d][...] = (keep[...].astype(F32) + got[...].astype(F32)).astype(BF16)


def join_kernel(count, place, mine, got, out):
    rows = out.shape[0] // count

    def fill(source):
        for d in range(count):
            at = pl.multiple_of(place[1 + d] * rows, rows)
            out[pl.ds(at, rows), :] = source[d * rows : (d + 1) * rows, :].astype(out.dtype)

    @pl.when(pl.program_id(0) == 0)
    def _():
        fill(mine)

    @pl.when(pl.program_id(0) == 1)
    def _():
        fill(got)


def join_blocks_kernel(count, place, mine, got, out):
    @pl.when(pl.program_id(0) < count)
    def _():
        out[...] = mine[...].astype(F32)

    @pl.when(pl.program_id(0) >= count)
    def _():
        out[...] = got[...].astype(F32)


def start_reduce(x, axis, size):
    near = lax.axis_index(axis) & 1
    rows = x.shape[0] // 2
    send = lax.dynamic_slice_in_dim(x, (1 - near) * rows, rows, 0)
    return x, send, partner(send, axis, size, 1)


def near_reduce(started, axis, size, after=()):
    x, _, got = started
    me = lax.axis_index(axis)
    near, far = me & 1, me >> 1
    count = size // 2
    rows, cols = x.shape[0] // size, x.shape[1]
    order = jnp.stack([far ^ d for d in range(count)])
    outs = [jax.ShapeDtypeStruct((rows, cols), BF16)] * count
    out_spec = pl.BlockSpec((rows, cols), lambda i, pr: (0, 0))
    waits = [pl.BlockSpec(memory_space=pl.ANY)] * len(after)
    if rows % 16 == 0:
        place = jnp.concatenate([near[None], order]).astype(jnp.int32)
        return pl.pallas_call(
            partial(spread_kernel, count),
            name="sr",
            cost_estimate=small_cost(3),
            out_shape=outs,
            grid_spec=pltpu.PrefetchScalarGridSpec(
                num_scalar_prefetch=1,
                grid=(1,),
                in_specs=[
                    pl.BlockSpec((rows * count, cols), lambda i, pr: (pr[0], 0)),
                    pl.BlockSpec((rows * count, cols), lambda i, pr: (0, 0)),
                ] + waits,
                out_specs=[out_spec] * count,
            ),
        )(place, x, got, *after)
    place = jnp.concatenate([near * count + order, order]).astype(jnp.int32)
    return pl.pallas_call(
        partial(spread_blocks_kernel, count),
        name="sr",
        cost_estimate=small_cost(3),
        out_shape=outs,
        grid_spec=pltpu.PrefetchScalarGridSpec(
            num_scalar_prefetch=1,
            grid=(count,),
            in_specs=[
                pl.BlockSpec((rows, cols), lambda i, pr: (pr[i], 0)),
                pl.BlockSpec((rows, cols), lambda i, pr: (pr[count + i], 0)),
            ] + waits,
            out_specs=[out_spec] * count,
        ),
    )(place, x, got, *after)


def add_kernel(count, *refs):
    total = refs[0][...].astype(F32)
    for d in range(1, count):
        total = total + refs[d][...].astype(F32)
    refs[-1][...] = total.astype(BF16)


def far_reduce(parts, axis, size, after=()):
    count = size // 2
    got = [parts[0]] + [partner(parts[d], axis, size, d << 1) for d in range(1, count)]
    spec = pl.BlockSpec(parts[0].shape, lambda: (0, 0))
    return pl.pallas_call(
        partial(add_kernel, count),
        name="ar",
        cost_estimate=small_cost(2),
        out_shape=jax.ShapeDtypeStruct(parts[0].shape, BF16),
        in_specs=[spec] * count + [pl.BlockSpec(memory_space=pl.ANY)] * len(after),
        out_specs=spec,
    )(*got, *after)


def gather_rows(x, axis, size):
    me = lax.axis_index(axis)
    near, far = me & 1, me >> 1
    count = size // 2
    rows, cols = x.shape
    mine = jnp.concatenate([x] + [partner(x, axis, size, d << 1) for d in range(1, count)], axis=0)
    got = partner(mine, axis, size, 1)
    order = jnp.stack([far ^ d for d in range(count)])
    if rows % 16 == 0:
        place = jnp.concatenate([near[None], order]).astype(jnp.int32)
        half = pl.BlockSpec((rows * count, cols), lambda i, pr: (0, 0))
        return pl.pallas_call(
            partial(join_kernel, count),
            name="jr",
            cost_estimate=small_cost(4),
            out_shape=jax.ShapeDtypeStruct((rows * size, cols), F32),
            grid_spec=pltpu.PrefetchScalarGridSpec(
                num_scalar_prefetch=1,
                grid=(2,),
                in_specs=[half, half],
                out_specs=pl.BlockSpec(
                    (rows * count, cols), lambda i, pr: (jnp.where(i == 0, pr[0], 1 - pr[0]), 0)
                ),
            ),
        )(place, mine, got)
    place = jnp.concatenate([near * count + order, (1 - near) * count + order])
    return pl.pallas_call(
        partial(join_blocks_kernel, count),
        name="jr",
        cost_estimate=small_cost(4),
        out_shape=jax.ShapeDtypeStruct((rows * size, cols), F32),
        grid_spec=pltpu.PrefetchScalarGridSpec(
            num_scalar_prefetch=1,
            grid=(size,),
            in_specs=[
                pl.BlockSpec((rows, cols), lambda i, pr: (jnp.minimum(i, count - 1), 0)),
                pl.BlockSpec((rows, cols), lambda i, pr: (jnp.maximum(i - count, 0), 0)),
            ],
            out_specs=pl.BlockSpec((rows, cols), lambda i, pr: (pr[i], 0)),
        ),
    )(place.astype(jnp.int32), mine, got)


def sum_doubling(x, axis, size, hop=F32):
    for b in range(bits_of(size)):
        low = x.astype(hop)
        x = low.astype(F32) + partner(low, axis, size, 1 << b).astype(F32)
    return x


def start_half(x, axis, size):
    mine = lax.axis_index(axis) & 1
    half = x.shape[0] // 2
    send = lax.dynamic_slice_in_dim(x, (1 - mine) * half, half, 0)
    return x, partner(send, axis, size, 1)


def near_half(started, axis, size):
    x, got = started
    mine = lax.axis_index(axis) & 1
    keep = lax.dynamic_slice_in_dim(x, mine * got.shape[0], got.shape[0], 0)
    low = (keep.astype(F32) + got.astype(F32)).astype(BF16)
    if bits_of(size) < 2:
        return None, low, None
    return size, low, partner(low, axis, size, 2)


def far_half(state, axis, size):
    _, low, got = state
    total = low.astype(F32)
    if got is not None:
        total = total + got.astype(F32)
    for b in range(2, bits_of(size)):
        low = total.astype(BF16)
        total = low.astype(F32) + partner(low, axis, size, 1 << b).astype(F32)
    return total


def share_half(x, axis, size):
    return x, partner(x, axis, size, 1)


def paste_kernel(place, own, got, out):
    @pl.when(pl.program_id(0) == place[0])
    def _():
        out[...] = own[...]

    @pl.when(pl.program_id(0) != place[0])
    def _():
        out[...] = got[...]


def paste_halves(own, got, me):
    rows, cols = own.shape
    half = pl.BlockSpec((rows, cols), lambda i, pr: (0, 0))
    return pl.pallas_call(
        paste_kernel,
        name="ph",
        cost_estimate=small_cost(4),
        out_shape=jax.ShapeDtypeStruct((rows * 2, cols), own.dtype),
        grid_spec=pltpu.PrefetchScalarGridSpec(
            num_scalar_prefetch=1,
            grid=(2,),
            in_specs=[half, half],
            out_specs=pl.BlockSpec((rows, cols), lambda i, pr: (i, 0)),
        ),
    )((me & 1).astype(jnp.int32).reshape(1), own, got)


def body(
    dp, tensor,
    hidden, segment_ids, norm_gain, gate_weight, input_weight, step_weight, state_weight,
    conv_weight, state_conv_weight, conv_bias, state_conv_bias, step_bias, decay_log,
    skip_gain, gate_norm_gain, out_weight, cotangent,
):
    tokens, model = hidden.shape
    channels = gate_weight.shape[1]
    heads = step_bias.shape[0]
    width = channels // heads
    state = state_weight.shape[1] // 2
    group = GROUP
    blocks = tokens // group
    me_t = lax.axis_index(TENSOR)
    side = (me_t & 1).astype(jnp.int32).reshape(1)

    seg_row = segment_ids.astype(F32).reshape(blocks, 1, group)
    pad = LANES - heads
    step_w = jnp.pad(step_weight, ((0, 0), (0, pad)))
    neg_a = -jnp.exp(decay_log)
    head_row = jnp.pad(
        jnp.stack([step_bias, neg_a * LOG2E, skip_gain, neg_a]), ((0, 4), (0, pad))
    )
    row2 = lambda v: v.reshape(1, -1)

    full = lambda shape: pl.BlockSpec(shape, lambda i, *_: (0,) * len(shape))
    once = lambda shape: pl.BlockSpec(
        shape, lambda i, *_: (0,) * len(shape), pipeline_mode=pl.Buffered(1)
    )
    tok = lambda cols: pl.BlockSpec((group, cols), lambda i, *_: (i, 0))
    segs = pl.BlockSpec((None, 1, group), lambda i, *_: (i, 0, 0))
    rev = lambda cols: pl.BlockSpec((group, cols), lambda i, *_: (blocks - 1 - i, 0))
    seg_rev = pl.BlockSpec((None, 1, group), lambda i, *_: (blocks - 1 - i, 0, 0))
    sds = jax.ShapeDtypeStruct
    cost = lambda us: pl.CostEstimate(
        flops=0, transcendentals=0, bytes_accessed=int(us * 3.3e6)
    )
    params = pltpu.CompilerParams(
        vmem_limit_bytes=60 * 1024 * 1024
    )

    (normed, gate_pre, u, z, state_z, state_u, states, step_pre, y, s_in, d_gn, sums) = pl.pallas_call(
        partial(forward_kernel, (group, channels, heads, width, state)),
        name="fs",
        cost_estimate=cost(40),
        out_shape=(
            sds((tokens, model), BF16),
            sds((tokens, channels), F32),
            sds((tokens, channels), BF16),
            sds((tokens, channels), F32),
            sds((tokens, 2 * state), F32),
            sds((tokens, 2 * state), F32),
            sds((tokens, 2 * state), BF16),
            sds((tokens, LANES), F32),
            sds((tokens, channels), F32),
            sds((blocks, state, channels), F32),
            sds((tokens, channels), F32),
            sds((blocks, 2, group), F32),
        ),
        grid_spec=pltpu.PrefetchScalarGridSpec(
            num_scalar_prefetch=1,
            grid=(blocks,),
            in_specs=[
                tok(model), segs, tok(model), once((1, model)),
                once((model, channels)), once((model, channels)), once((model, 2 * state)),
                once((model, LANES)), once((4, channels)), once((1, channels)),
                once((4, 2 * state)), once((1, 2 * state)), once((8, LANES)),
                once((1, channels)), once((channels, model)),
            ],
            out_specs=[
                tok(model), tok(channels), tok(channels), tok(channels), tok(2 * state),
                tok(2 * state), tok(2 * state), tok(LANES), tok(channels),
                pl.BlockSpec((None, state, channels), lambda i, *_: (i, 0, 0)),
                tok(channels),
                pl.BlockSpec((None, 2, group), lambda i, *_: (i, 0, 0)),
            ],
            scratch_shapes=[
                pltpu.VMEM((group + 8, channels), F32),
                pltpu.VMEM((group + 8, 2 * state), F32),
                pltpu.VMEM((group + 8, LANES), F32),
                pltpu.VMEM((state, channels), F32),
                pltpu.VMEM((LANES, group), F32),
                pltpu.VMEM((group, LANES), F32),
                pltpu.VMEM((group, group), F32),
                pltpu.VMEM((group, channels), BF16),
            ],
        ),
        compiler_params=params,
    )(
        segment_ids, hidden, seg_row, cotangent, row2(norm_gain), gate_weight, input_weight,
        state_weight, step_w, conv_weight, row2(conv_bias), state_conv_weight,
        row2(state_conv_bias), head_row, row2(gate_norm_gain), out_weight,
    )

    sums = sum_doubling(sums, TENSOR, tensor)
    gnormed, d_y, d_gate, grad_gnorm = pl.pallas_call(
        partial(gate_kernel, (group, channels, float(channels * tensor))),
        name="gt",
        cost_estimate=cost(10),
        out_shape=(
            sds((tokens, channels), BF16), sds((tokens, channels), BF16),
            sds((tokens, channels), BF16), sds((8, channels), F32),
        ),
        grid_spec=pl.GridSpec(
            grid=(blocks,),
            in_specs=[
                pl.BlockSpec((None, 2, group), lambda i: (i, 0, 0)), segs,
                tok(channels), tok(channels), tok(channels), full((1, channels)),
            ],
            out_specs=[tok(channels), tok(channels), tok(channels), full((8, channels))],
        ),
        compiler_params=params,
    )(sums, seg_row, y, gate_pre, d_gn, row2(gate_norm_gain))

    g_out = start_reduce(mm(gnormed, cotangent, TN).astype(BF16), DP, dp)
    mix = mm(gnormed, out_weight).astype(BF16)
    mix = start_half(mix, TENSOR, tensor)
    g_gate = mm(normed, d_gate, TN).astype(BF16)
    g_gate = start_reduce(g_gate, DP, dp)

    part = channels

    def backward(k, waits):
        revc = pl.BlockSpec((group, part), lambda i, *_: (blocks - 1 - i, k))
        return pl.pallas_call(
            partial(
                backward_kernel,
                (group, part, k * (heads // 2), width, state, blocks, len(waits)),
            ),
            name="bs",
            cost_estimate=cost(42),
            out_shape=(
                sds((tokens, part), BF16), sds((tokens, LANES), BF16),
                sds((tokens, 2 * state), BF16), sds((8, part), F32),
                sds((8, part), F32), sds((8, LANES), F32),
            ),
            grid_spec=pltpu.PrefetchScalarGridSpec(
                num_scalar_prefetch=1,
                grid=(blocks,),
                in_specs=[
                    seg_rev, revc, revc, revc, revc, rev(2 * state), rev(LANES),
                    pl.BlockSpec((None, state, part), lambda i, *_: (blocks - 1 - i, 0, k)),
                    pl.BlockSpec((4, part), lambda i, *_: (0, k)), once((8, LANES)),
                ] + [pl.BlockSpec(memory_space=pl.ANY)] * len(waits),
                out_specs=[
                    rev(part), rev(LANES), rev(2 * state),
                    full((8, part)), full((8, part)), full((8, LANES)),
                ],
                scratch_shapes=[
                    pltpu.VMEM((group + 8, part), F32),
                    pltpu.VMEM((group + 8, LANES), F32),
                    pltpu.VMEM((state, part), F32),
                    pltpu.VMEM((8, LANES), F32),
                    pltpu.VMEM((LANES, group), F32),
                    pltpu.VMEM((group, LANES), F32),
                    pltpu.VMEM((group, group), F32),
                    pltpu.VMEM((group, group), F32),
                    pltpu.VMEM((group, part), BF16),
                    pltpu.VMEM((group, part), BF16),
                    pltpu.VMEM((state, part), BF16),
                ],
            ),
            compiler_params=params,
        )(
            segment_ids, seg_row, d_y, y, z, u, states, step_pre, s_in, conv_weight, head_row,
            *waits,
        )

    mix = near_half(mix, TENSOR, tensor)
    g_out = near_reduce(g_out, DP, dp, [mix[1], g_gate[1]])
    d_input, d_step, d_states, grad_conv, grad_cb, grad_head = backward(
        0, [g_out[1]]
    )

    states_half = far_half(
        near_half(start_half(d_states, TENSOR, tensor), TENSOR, tensor), TENSOR, tensor,
    ).astype(BF16)
    g_in = start_reduce(mm(normed, d_input, TN).astype(BF16), DP, dp)
    g_out = far_reduce(g_out, DP, dp, [d_step])
    g_gate = near_reduce(g_gate, DP, dp, [d_step])
    local_back = pl.pallas_call(
        project_kernel,
        name="pb",
        cost_estimate=cost(10),
        out_shape=sds((tokens, model), BF16),
        grid_spec=pl.GridSpec(
            grid=(blocks,),
            in_specs=[
                tok(channels), tok(channels), tok(LANES),
                once((model, channels)), once((model, channels)), once((model, LANES)),
            ] + [pl.BlockSpec(memory_space=pl.ANY)] * 3,
            out_specs=tok(model),
        ),
        compiler_params=params,
    )(
        d_gate, d_input, d_step, gate_weight, input_weight, step_w,
        g_in[1], g_gate[1], g_out,
    )
    back_half = near_half(start_half(local_back, TENSOR, tensor), TENSOR, tensor)
    mix_half = far_half(mix, TENSOR, tensor)
    d_states = share_half(states_half, TENSOR, tensor)
    low = back_half[1]
    g_gate = far_reduce(g_gate, DP, dp, [low])
    g_in = near_reduce(g_in, DP, dp, [low])
    g_in = far_reduce(g_in, DP, dp)
    back_half = far_half(back_half, TENSOR, tensor).astype(BF16)

    state_b, grad_sconv, grad_scb = pl.pallas_call(
        partial(state_kernel, (group, 2 * state, blocks)),
        name="sc",
        cost_estimate=cost(6),
        out_shape=(
            sds((tokens, 2 * state), BF16), sds((8, 2 * state), F32), sds((8, 2 * state), F32),
        ),
        grid_spec=pltpu.PrefetchScalarGridSpec(
            num_scalar_prefetch=1,
            grid=(blocks,),
            in_specs=[
                seg_rev,
                pl.BlockSpec((group, 2 * state), lambda i, *_: (lax.rem(blocks - 1 - i, blocks // 2), 0)),
                pl.BlockSpec((group, 2 * state), lambda i, *_: (lax.rem(blocks - 1 - i, blocks // 2), 0)),
                rev(2 * state), rev(2 * state), full((4, 2 * state)),
            ],
            out_specs=[rev(2 * state), full((8, 2 * state)), full((8, 2 * state))],
            scratch_shapes=[
                pltpu.VMEM((group + 8, 2 * state), F32), pltpu.VMEM((group + 8, LANES), F32),
            ],
        ),
        compiler_params=params,
    )(side, seg_row, *d_states, state_z, state_u, state_conv_weight)

    rows_t = model // tensor
    normed_part = lax.dynamic_slice_in_dim(normed, me_t * rows_t, rows_t, 1)
    g_state = mm(normed_part, state_b, TN)
    grad_step = mm(d_step, normed, TN)[:16]

    rows = tokens // 2
    hid_half = lax.dynamic_slice_in_dim(hidden, (me_t & 1) * rows, rows, 0)
    out_half = (hid_half.astype(F32) + mix_half).astype(BF16)
    block_out = paste_halves(*share_half(out_half, TENSOR, tensor), me_t)
    back = share_half(back_half, TENSOR, tensor)

    own_first = lambda cols: pl.BlockSpec(
        (group, cols), lambda i, pr: (lax.rem(i + pr[0] * (blocks // 2), blocks), 0)
    )
    grad_hidden, grad_norm = pl.pallas_call(
        partial(final_kernel, blocks // 2),
        name="fg",
        cost_estimate=cost(12),
        out_shape=(sds((tokens, model), F32), sds((8, model), F32)),
        grid_spec=pltpu.PrefetchScalarGridSpec(
            num_scalar_prefetch=1,
            grid=(blocks,),
            in_specs=[
                pl.BlockSpec((group, model), lambda i, pr: (jnp.minimum(i, blocks // 2 - 1), 0)),
                pl.BlockSpec((group, model), lambda i, pr: (jnp.maximum(i - blocks // 2, 0), 0)),
                own_first(2 * state), full((model, 2 * state)), own_first(model),
                own_first(model), full((1, model)),
            ],
            out_specs=[own_first(model), full((8, model))],
        ),
        compiler_params=params,
    )(side, *back, state_b, state_weight, hidden, cotangent, row2(norm_gain))

    grad_out = gather_rows(g_out, DP, dp)
    grad_gate = gather_rows(g_gate, DP, dp)
    grad_input = gather_rows(g_in, DP, dp)

    def line(*parts):
        flat = jnp.concatenate([v.reshape(1, -1) for v in parts], axis=1)
        fill = -flat.shape[1] % model
        return jnp.pad(flat, ((0, 0), (0, fill))).reshape(-1, model)

    taps = conv_weight.shape[0]
    small = jnp.concatenate(
        [
            grad_step,
            line(grad_conv[:taps]),
            line(grad_cb[0:1], grad_gnorm[0:1]),
            line(grad_sconv[:taps], grad_scb[0:1]),
            line(grad_head[0:3]),
        ],
        axis=0,
    )
    fill = -small.shape[0] % 8
    small = jnp.pad(small, ((0, fill), (0, 0)))
    lines = small.shape[0]
    small = sum_doubling(jnp.concatenate([small, g_state.reshape(-1, model)], axis=0), DP, dp, BF16)
    g_state = small[lines:].reshape(rows_t, 2 * state).astype(BF16)
    grad_norm = sum_doubling(grad_norm, DP, dp)[0]
    pieces = [g_state]
    for b in range(bits_of(tensor)):
        low = (me_t >> b) & 1
        pieces = [
            jnp.where(low == 0, jnp.concatenate([v, w]), jnp.concatenate([w, v]))
            for v, w in ((v, partner(v, TENSOR, tensor, 1 << b)) for v in pieces)
        ]
    grad_state = pieces[0].astype(F32)

    flat = small.reshape(-1)
    at = 0

    def take(count, shape):
        nonlocal at
        out = flat[at : at + count].reshape(shape)
        at += count
        return out

    def align():
        nonlocal at
        at += -at % model

    grad_step = small[:heads].T
    at = 16 * model
    grad_conv = take(taps * channels, (taps, channels))
    align()
    grad_cb = take(channels, (channels,))
    grad_gnorm = take(channels, (channels,))
    align()
    grad_sconv = take(taps * 2 * state, (taps, 2 * state))
    grad_scb = take(2 * state, (2 * state,))
    align()
    heads_out = take(3 * LANES, (3, LANES))
    grad_sbias, grad_decay, grad_skip = (heads_out[k, :heads] for k in range(3))
    return (
        block_out, grad_hidden, grad_norm, grad_gate, grad_input, grad_step, grad_state,
        grad_conv, grad_sconv, grad_cb, grad_scb, grad_sbias, grad_decay, grad_skip,
        grad_gnorm, grad_out,
    )


def solution(mesh):
    return jax.shard_map(
        partial(body, mesh.shape[DP], mesh.shape[TENSOR]),
        mesh=mesh,
        in_specs=(
            P(DP, None), P(DP), P(), P(None, TENSOR), P(None, TENSOR),
            P(None, TENSOR), P(), P(None, TENSOR), P(), P(TENSOR), P(), P(TENSOR),
            P(TENSOR), P(TENSOR), P(TENSOR), P(TENSOR, None), P(DP, None),
        ),
        out_specs=(
            P(DP, None), P(DP, None), P(), P(None, TENSOR), P(None, TENSOR),
            P(None, TENSOR), P(), P(None, TENSOR), P(), P(TENSOR), P(), P(TENSOR),
            P(TENSOR), P(TENSOR), P(TENSOR), P(TENSOR, None),
        ),
        check_vma=False,
    )
```
